128 devices in a mesh: pool: 4 (over z), ka: 32 (over x, y, core).
Axes of the slice: x: 4, y: 4, z: 4, core: 2. Of those that a mesh axis runs over, the one named last changes fastest.
Arguments:
- rates: bfloat16 [32768, 4096], P(('pool', 'ka')), may hold values from -0.09375 to 0.09375
- tile_dest: int32 [32768, 1], P(('pool', 'ka')), may hold values from 0 to 127; in each aligned block of 256 rows (0 to 255, 256 to 511, ...) at most 4 rows name the same one
- tile_row: int32 [32768], P(('pool', 'ka')), may hold values from 0 to 3
- tile_col: int32 [32768], P(('pool', 'ka')), may hold values from 0 to 127
- send_list: int32 [128, 128], P(('pool', 'ka')), may hold values from 0 to 3
- drive: float32 [512, 12288], P(('pool', 'ka')), may hold values from -6 to 6
- tau: float32 [512, 4096], P(('pool', 'ka')), may hold values from 0.2 to 1
Outputs:
- population: float32 [512, 12288], P(('pool', 'ka'))
The draws below stay inside these ranges and needn't reach their ends.
Inputs may be any that keep to these rules, and one draw needn't show every extreme that they name: `tile_dest`: owner device of the tile's k-row block; among the 256 tiles of one device no owner is named more than 4 times. `tile_col`: names the device that lists the tile's k+q column block for the tile's owner. `send_list`: entry [s, d] is the local k block of device s that owner d reads as column entry s.
All inputs are finite; a program needn't handle non-finite values.
Results may differ from the reference program's by a relative error of at most 0.0025.
Values may be sent and summed in bfloat16 or wider, within the bound.
No kernel may reach another device: no remote copies, remote signals or barrier semaphores. Data moves between devices by JAX's collectives and lax.ppermute only.
A program may use at most 64 MiB of HBM per device.

```python
import math
import jax
import jax.numpy as jnp
import numpy as np
from jax import lax

B = 64
NPT = 64
KB_DEV = 4
PER_BLOCK = 64
ITERS = 3
TILES_DEV = 256
TILES = 32768
CAP = 4
NB = 512
N_POOL = 4
N_KA = 32


def plant(array, key, smallest, largest):
    index_at = [jax.random.randint(jax.random.fold_in(key, axis), (), 0, length) for axis, length in enumerate(array.shape)]
    longest = array.shape.index(max(array.shape))
    next_to = index_at[:longest] + [(index_at[longest] + 1) % array.shape[longest]] + index_at[longest + 1:]
    return array.at[tuple(index_at)].set(smallest).at[tuple(next_to)].set(largest)


def shard_levels(rng, shape, pieces, smallest, high):
    def one(position, shards_of):
        steps = jax.random.uniform(jax.random.fold_in(jax.random.fold_in(rng, 6), position), (shards_of,), jnp.float32, smallest / len(pieces), high / len(pieces))
        return jnp.repeat(jnp.exp(steps), shape[position] // shards_of).reshape((-1,) + (1,) * (len(shape) - position - 1))

    level = one(*pieces[0])
    for cut in pieces[1:]:
        level = level * one(*cut)
    return level


def routed_block(stream_key, own, number, rows, amount, top, bound, skew):
    order = jax.random.permutation(stream_key, amount)
    crowded, usual = shares(amount, rows * top, bound, skew, True), shares(amount, rows * top, bound, skew, False)
    places = jnp.arange(amount)

    def named(lengths, rotation):
        used = int((lengths > 0).sum())
        fixed = max(1, used // 4)
        shifted = fixed + (places - fixed + rotation * (used - fixed)) % max(1, amount - fixed)
        return jnp.zeros((amount,), jnp.int32).at[order[jnp.where(places < fixed, places, shifted)]].set(jnp.asarray(lengths, jnp.int32))

    lengths = jnp.where(number % 4 == 0, named(crowded, number // 4), named(usual, number - number // 4 - 1))
    mixed = jax.random.permutation(jax.random.fold_in(own, 3), amount)
    donor, taker = mixed[0:amount // 2 * 2:2], mixed[1:amount // 2 * 2:2]
    slack = jnp.minimum(lengths[donor] - 1, bound - lengths[taker]) // 2
    slack = jnp.where((donor == order[0]) | (taker == order[0]) | (lengths[taker] == 0), 0, jnp.maximum(slack, 0))
    shifted = jax.random.randint(jax.random.fold_in(own, 4), (amount // 2,), 0, 1 << 20) % (slack + 1)
    lengths = lengths.at[donor].add(-shifted).at[taker].add(shifted)
    items = jnp.searchsorted(jnp.cumsum(lengths), jnp.arange(rows * top), side="right").astype(jnp.int32)
    grid = items.reshape(top, rows).T
    grid = grid[jax.random.permutation(jax.random.fold_in(own, 1), rows)]
    rotation = jax.random.randint(jax.random.fold_in(own, 2), (rows, 1), 0, top)
    return jnp.take_along_axis(grid, (jnp.arange(top)[None, :] + rotation) % top, axis=1)


def shares(amount, total, bound, skew, full):
    weights = [(1 << 20) // math.isqrt(standing ** skew) + 1 for standing in range(1, amount + 1)]
    largest = bound if full else min(bound, max(-(-total // amount), total * weights[0] // sum(weights)))
    least = 1 if total - largest >= amount - 1 else 0
    given, spare = [largest] + [least] * (amount - 1), total - largest - least * (amount - 1)
    while spare > 0:
        movable = [i for i in range(1, amount) if given[i] < largest] or [i for i in range(1, amount) if given[i] < bound]
        whole, remaining = sum([weights[i] for i in movable]), spare
        for i in movable:
            more = min(bound - given[i], max(1, remaining * weights[i] // whole), spare)
            given[i] = given[i] + more
            spare = spare - more
    return np.array(given)


def bell_draw(key, extent, scale, limit, pieces=(), held_as=jnp.bfloat16):
    array = scale * jax.random.normal(key, extent, jnp.float32)
    if pieces:
        array = array * shard_levels(key, extent, pieces, -0.22, 0.18)
    return jnp.clip(array, -limit, limit).astype(held_as)


def setup_inputs(seed: int = 0) -> dict:
    keys = jax.random.split(jax.random.key(seed), 8)
    rates = bell_draw(keys[0], (TILES, B * B), (B * PER_BLOCK) ** -0.5, 0.09375, ((0, 128),))
    tile_dest_keys = jax.random.split(jax.random.fold_in(keys[1], 1), TILES // TILES_DEV)
    tile_dest_turns = jax.random.permutation(jax.random.fold_in(keys[1], 3), TILES // TILES_DEV)
    tile_dest = jax.vmap(lambda own, number: routed_block(jax.random.fold_in(keys[1], 2), own, number, TILES_DEV, N_POOL * N_KA, 1, CAP, 2))(tile_dest_keys, tile_dest_turns).reshape((TILES, 1))
    tile_row = plant(jax.random.randint(keys[2], (TILES,), 0, KB_DEV), jax.random.fold_in(keys[2], 1), 0, KB_DEV - 1).astype(jnp.int32)
    tile_col = plant(jax.random.randint(keys[3], (TILES,), 0, N_POOL * N_KA), jax.random.fold_in(keys[3], 1), 0, (N_POOL * N_KA) - 1).astype(jnp.int32)
    send_list = plant(jax.random.randint(keys[4], (N_POOL * N_KA, N_POOL * N_KA), 0, KB_DEV), jax.random.fold_in(keys[4], 1), 0, KB_DEV - 1).astype(jnp.int32)
    drive = bell_draw(keys[5], (NB, 3 * B * NPT), 1.0, 6.0, ((0, 128),), jnp.float32)
    tau = jnp.clip(jnp.exp(math.log(1.0) - 1.609438 * jax.random.uniform(keys[6], (NB, B * NPT), jnp.float32) ** shard_levels(keys[6], (NB, B * NPT), ((0, 128),), -0.2, 0.2)), 0.2, 1.0)
    return dict(rates=rates, tile_dest=tile_dest, tile_row=tile_row, tile_col=tile_col, send_list=send_list, drive=drive, tau=tau)


def reference(rates, tile_dest, tile_row, tile_col, send_list, drive, tau):
    members = N_POOL * N_KA
    all_slots = members * CAP
    tiles3 = rates.reshape(TILES, B, B)
    owner_of = tile_dest[:, 0].astype(jnp.int32)
    by_owner = jnp.argsort(owner_of, stable=True).astype(jnp.int32)
    sources = jnp.arange(members, dtype=jnp.int32)
    counts = jnp.sum((owner_of[:, None] == sources[None, :]).astype(jnp.int32), axis=0)
    starts = (jnp.cumsum(counts) - counts).astype(jnp.int32)
    pairs_all = (tile_row * members + tile_col).astype(jnp.int32)
    drive4 = drive.reshape(NB, 3, B, NPT)
    tau4 = tau.reshape(NB, 1, B, NPT)

    def assemble(owner):
        places = jnp.arange(all_slots, dtype=jnp.int32)
        filled = places < counts[owner]
        picked = by_owner[jnp.minimum(starts[owner] + places, TILES - 1)]
        tile_data = jnp.where(filled[:, None, None], tiles3[picked].astype(jnp.float32), jnp.float32(0.0))
        pair_ids = jnp.where(filled, pairs_all[picked], 0).astype(jnp.int32)
        summed = jnp.zeros((KB_DEV * members, B, B), jnp.float32).at[pair_ids].add(tile_data)
        return summed.astype(jnp.bfloat16).reshape(KB_DEV, members, B, B)

    def apply_rates(packed):
        def per_owner(owner):
            operator = assemble(owner)
            columns = (sources * KB_DEV + send_list[:, owner]).astype(jnp.int32)
            blocks = packed[columns]
            return jnp.einsum('rjab,jnbp->rnap', operator.astype(jnp.float32), blocks.astype(jnp.float32), precision=lax.Precision.HIGHEST)
        return lax.map(per_owner, sources).reshape(NB, 3, B, NPT)

    population = drive4
    for sweep in range(ITERS):
        packed = population.astype(jnp.bfloat16)
        population = drive4 + tau4 * apply_rates(packed)
    return population.reshape(NB, 3 * B * NPT)
```

```python
import functools

import jax
import jax.numpy as jnp
from jax import lax
from jax.experimental import pallas as pl
from jax.experimental.pallas import tpu as pltpu
from jax.sharding import PartitionSpec as P

ROWS = 32
LANES = 128
HALF = 64
ITERS = 3
CAP = 4
DIRS = 3
AXES = ("pool", "ka")
TILE_ROWS = CAP * ROWS
BLOCK_ROWS = DIRS * ROWS
LABEL_AT = TILE_ROWS + BLOCK_ROWS
FIRST_ROWS = LABEL_AT + 8

VMEM = pltpu.MemorySpace.VMEM
SMEM = pltpu.MemorySpace.SMEM


def vspec():
    return pl.BlockSpec(memory_space=VMEM)


def sspec():
    return pl.BlockSpec(memory_space=SMEM)


def params(mib):
    return pltpu.CompilerParams(vmem_limit_bytes=mib << 20)


def fill_kernel(dest_ref, row_ref, col_ref, sel_ref, rates_ref, drive_ref, out_ref, perm_ref, cnt_ref, lab_ref, pk_ref):
    members = out_ref.shape[0]
    tiles = rates_ref.shape[0]
    lane = lax.broadcasted_iota(jnp.int32, (1, LANES), 1)
    lab_ref[...] = jnp.full(lab_ref.shape, 4 * members, jnp.int32)
    pk_ref[...] = drive_ref[...].astype(jnp.bfloat16)

    def block(d, carry):
        cnt_ref[d] = 0
        out_ref[d, TILE_ROWS:LABEL_AT, :] = pk_ref[sel_ref[d]]
        return carry

    lax.fori_loop(0, members, block, 0, unroll=8)

    def place(i, carry):
        d = dest_ref[i]
        c = cnt_ref[d]
        cnt_ref[d] = c + 1
        where = row_ref[i] * members + col_ref[i]
        lab_ref[d] = jnp.where(lane == c, where, lab_ref[d])
        out_ref[d, pl.ds(pl.multiple_of(c * ROWS, ROWS), ROWS), :] = rates_ref[i]
        return carry

    lax.fori_loop(0, tiles, place, 0, unroll=4)

    sub = lax.broadcasted_iota(jnp.int32, (8, LANES), 0)

    def label(d, carry):
        value = jnp.broadcast_to(lab_ref[d], (8, LANES))
        value = jnp.where(sub == 0, value >> 3, value & 7)
        out_ref[d, LABEL_AT:FIRST_ROWS, :] = value.astype(jnp.float32).astype(jnp.bfloat16)
        return carry

    lax.fori_loop(0, members, label, 0, unroll=4)

    size = perm_ref.shape[0]
    k = lax.broadcasted_iota(jnp.int32, (size, size), 0)
    m = lax.broadcasted_iota(jnp.int32, (size, size), 1)
    want = ((m >> 5) & 3) * LANES + (m >> 8) * HALF + 2 * (m & 31) + ((m >> 7) & 1)
    perm_ref[...] = (k == want).astype(jnp.float32).astype(jnp.bfloat16)


def advance(last, op_ref, x_ref, x_at, sel_ref, drive_ref, tau_ref, out_ref, pk_ref):
    members = x_ref.shape[0]
    kblocks = drive_ref.shape[0]
    depth = members * ROWS
    right = [x_ref[:, x_at + n * ROWS : x_at + (n + 1) * ROWS, :].reshape(depth, LANES) for n in range(DIRS)]
    total = jnp.dot(op_ref[...], jnp.concatenate(right, axis=1), preferred_element_type=jnp.float32)
    low = lax.broadcasted_iota(jnp.int32, (ROWS, LANES), 1) < HALF
    for n in range(DIRS):
        for r in range(kblocks):

            def part(hb, ha):
                at = hb * 256 + r * HALF + ha * ROWS
                return total[at : at + ROWS, n * LANES : (n + 1) * LANES]

            same = jnp.where(low, part(0, 0), part(1, 1))
            other = jnp.where(low, part(0, 1), part(1, 0))
            summed = same + pltpu.roll(other, HALF, 1)
            rows = slice(n * ROWS, (n + 1) * ROWS)
            new = drive_ref[r, rows, :] + tau_ref[r] * summed
            if last:
                out_ref[r, rows, :] = new
            else:
                pk_ref[r, rows, :] = new.astype(jnp.bfloat16)
    if not last:

        def block(d, carry):
            out_ref[d] = pk_ref[sel_ref[d]]
            return carry

        lax.fori_loop(0, members, block, 0, unroll=8)


def first_kernel(sel_ref, x_ref, perm_ref, drive_ref, tau_ref, op_ref, out_ref, acc_ref, lab_ref, at_ref, pk_ref, sem):
    members = x_ref.shape[0]

    def read(s, carry):
        value = x_ref[s, LABEL_AT:FIRST_ROWS, :].astype(jnp.float32)
        lab_ref[pl.ds(s, 1), :] = (value[0:1] * 8.0 + value[1:2]).astype(jnp.int32)
        return carry

    lax.fori_loop(0, members, read, 0, unroll=8)
    copy = pltpu.make_async_copy(lab_ref, at_ref, sem)
    copy.start()
    acc_ref[...] = jnp.zeros_like(acc_ref)
    copy.wait()

    def add(s, carry):
        for c in range(CAP):
            tile = x_ref[s, c * ROWS : (c + 1) * ROWS, :].astype(jnp.float32)
            at = at_ref[s, c]
            acc_ref[at] = acc_ref[at] + tile
        return carry

    lax.fori_loop(0, members, add, 0, unroll=2)

    groups = members // 4
    chunk = 8

    def turn(r, carry):
        for g0 in range(0, groups, chunk):
            parts = [[] for _ in range(4)]
            for g in range(g0, g0 + chunk):
                for q in range(4):
                    parts[q].append(acc_ref[r * members + g * 4 + q].astype(jnp.bfloat16))
            left = jnp.concatenate([jnp.concatenate(p, axis=0) for p in parts], axis=1)
            out = jnp.dot(left, perm_ref[...], preferred_element_type=jnp.float32).astype(jnp.bfloat16)
            for ha in range(2):
                for hb in range(2):
                    at = pl.multiple_of(hb * 256 + r * HALF + ha * ROWS, ROWS)
                    piece = out[:, (ha * 2 + hb) * LANES : (ha * 2 + hb + 1) * LANES]
                    for g in range(chunk):
                        op_ref[pl.ds(at, ROWS), (g0 + g) * LANES : (g0 + g + 1) * LANES] = piece[g * ROWS : (g + 1) * ROWS]
        return carry

    lax.fori_loop(0, 4, turn, 0)
    advance(False, op_ref, x_ref, TILE_ROWS, sel_ref, drive_ref, tau_ref, out_ref, pk_ref)


def step_kernel(last, sel_ref, x_ref, op_ref, drive_ref, tau_ref, out_ref, *scratch):
    advance(last, op_ref, x_ref, 0, sel_ref, drive_ref, tau_ref, out_ref, scratch[0] if scratch else None)


def shards(rates, tile_dest, tile_row, tile_col, send_list, drive, tau):
    members = lax.axis_size("pool") * lax.axis_size("ka")
    tiles = rates.shape[0]
    kblocks = drive.shape[0]
    exchange = functools.partial(lax.all_to_all, axis_name=AXES, split_axis=0, concat_axis=0, tiled=True)
    bf16, f32, i32 = jnp.bfloat16, jnp.float32, jnp.int32
    packed = pltpu.VMEM((kblocks, BLOCK_ROWS, LANES), bf16)

    sel = send_list.reshape(members)
    drive3 = drive.reshape(kblocks, BLOCK_ROWS, LANES)
    tau3 = tau.reshape(kblocks, ROWS, LANES)

    first, perm = pl.pallas_call(
        fill_kernel,
        out_shape=[
            jax.ShapeDtypeStruct((members, FIRST_ROWS, LANES), bf16),
            jax.ShapeDtypeStruct((4 * LANES, 4 * LANES), bf16),
        ],
        in_specs=[sspec()] * 4 + [vspec()] * 2,
        out_specs=[vspec()] * 2,
        scratch_shapes=[pltpu.SMEM((members,), i32), pltpu.VMEM((members, 1, LANES), i32), packed],
        compiler_params=params(16),
        name="fill",
    )(tile_dest[:, 0], tile_row, tile_col, sel, rates.reshape(tiles, ROWS, LANES), drive3)
    first, tau3 = lax.optimization_barrier((first, tau3))
    first = exchange(first)

    operator, send = pl.pallas_call(
        first_kernel,
        out_shape=[
            jax.ShapeDtypeStruct((4 * LANES, members * ROWS), bf16),
            jax.ShapeDtypeStruct((members, BLOCK_ROWS, LANES), bf16),
        ],
        in_specs=[sspec()] + [vspec()] * 4,
        out_specs=[vspec()] * 2,
        scratch_shapes=[
            pltpu.VMEM((kblocks * members + 1, ROWS, LANES), f32),
            pltpu.VMEM((members, LANES), i32),
            pltpu.SMEM((members, LANES), i32),
            packed,
            pltpu.SemaphoreType.DMA(()),
        ],
        compiler_params=params(32),
        name="first",
    )(sel, first, perm, drive3, tau3)

    for sweep in range(1, ITERS):
        last = sweep == ITERS - 1
        shape = (kblocks, BLOCK_ROWS, LANES) if last else (members, BLOCK_ROWS, LANES)
        send = pl.pallas_call(
            functools.partial(step_kernel, last),
            out_shape=jax.ShapeDtypeStruct(shape, f32 if last else bf16),
            in_specs=[sspec()] + [vspec()] * 4,
            out_specs=vspec(),
            scratch_shapes=[] if last else [packed],
            compiler_params=params(20),
            name="step_last" if last else "step",
        )(sel, exchange(send), operator, drive3, tau3)
    return send.reshape(kblocks, BLOCK_ROWS * LANES)


def solution(mesh):
    pair = P(AXES, None)
    placed = (pair, pair, P(AXES), P(AXES), pair, pair, pair)
    return jax.shard_map(shards, mesh=mesh, in_specs=placed, out_specs=pair, check_vma=False)
```

```python
import functools

import jax
import jax.numpy as jnp
from jax import lax
from jax.experimental import pallas as pl
from jax.experimental.pallas import tpu as pltpu
from jax.sharding import PartitionSpec as P

ROWS = 32
LANES = 128
HALF = 64
ITERS = 3
CAP = 4
DIRS = 3
AXES = ("pool", "ka")
TILE_ROWS = CAP * ROWS
BLOCK_ROWS = DIRS * ROWS
LABEL_AT = TILE_ROWS + BLOCK_ROWS
FIRST_ROWS = LABEL_AT + 8

VMEM = pltpu.MemorySpace.VMEM
SMEM = pltpu.MemorySpace.SMEM


def vspec():
    return pl.BlockSpec(memory_space=VMEM)


def sspec():
    return pl.BlockSpec(memory_space=SMEM)


def params(mib):
    return pltpu.CompilerParams(vmem_limit_bytes=mib << 20)


def turned(value):
    return pltpu.roll(value, HALF, 1)


def fill_kernel(
    dest_ref, row_ref, col_ref, sel_ref, rates_ref, drive_ref, tau_ref, out_ref, perm_ref, du_ref, tu_ref, cnt_ref, lab_ref, pk_ref, nat_ref
):
    members = out_ref.shape[0]
    tiles = rates_ref.shape[0]
    kblocks = drive_ref.shape[0]
    lane = lax.broadcasted_iota(jnp.int32, (1, LANES), 1)
    low = lax.broadcasted_iota(jnp.int32, (ROWS, LANES), 1) < HALF
    lab_ref[...] = jnp.full(lab_ref.shape, 4 * members, jnp.int32)

    for k in range(kblocks):
        for c in range(BLOCK_ROWS):
            nat_ref[k, c : c + 1, :] = drive_ref[k : k + 1, c * LANES : (c + 1) * LANES]
        for c in range(ROWS):
            nat_ref[k, BLOCK_ROWS + c : BLOCK_ROWS + c + 1, :] = tau_ref[k : k + 1, c * LANES : (c + 1) * LANES]
    for k in range(kblocks):
        n0, n1, n2, t = (nat_ref[k, n * ROWS : (n + 1) * ROWS, :] for n in range(DIRS + 1))
        du_ref[k, 0:ROWS, :] = jnp.where(low, n0, turned(n1))
        du_ref[k, ROWS : 2 * ROWS, :] = jnp.where(low, turned(n0), n1)
        du_ref[k, 2 * ROWS :, :] = n2
        tu_ref[k, 0:ROWS, :] = jnp.where(low, t, turned(t))
        tu_ref[k, ROWS : 2 * ROWS, :] = jnp.where(low, turned(t), t)
        tu_ref[k, 2 * ROWS :, :] = t
    pk_ref[...] = du_ref[...].astype(jnp.bfloat16)

    def block(d, carry):
        cnt_ref[d] = 0
        out_ref[d, TILE_ROWS:LABEL_AT, :] = pk_ref[sel_ref[d]]
        return carry

    lax.fori_loop(0, members, block, 0, unroll=8)

    def place(i, carry):
        d = dest_ref[i]
        c = cnt_ref[d]
        cnt_ref[d] = c + 1
        where = row_ref[i] * members + col_ref[i]
        lab_ref[d] = jnp.where(lane == c, where, lab_ref[d])
        out_ref[d, pl.ds(pl.multiple_of(c * ROWS, ROWS), ROWS), :] = rates_ref[i]
        return carry

    lax.fori_loop(0, tiles, place, 0, unroll=4)

    sub = lax.broadcasted_iota(jnp.int32, (8, LANES), 0)

    def label(d, carry):
        value = jnp.broadcast_to(lab_ref[d], (8, LANES))
        value = jnp.where(sub == 0, value >> 3, value & 7)
        out_ref[d, LABEL_AT:FIRST_ROWS, :] = value.astype(jnp.float32).astype(jnp.bfloat16)
        return carry

    lax.fori_loop(0, members, label, 0, unroll=4)

    size = perm_ref.shape[0]
    m = lax.broadcasted_iota(jnp.int32, (1, size), 1)
    want = ((m >> 5) & 3) * LANES + (m >> 8) * HALF + 2 * (m & 31) + ((m >> 7) & 1)
    k = lax.broadcasted_iota(jnp.int32, (ROWS, size), 0)
    for at in range(0, size, ROWS):
        perm_ref[at : at + ROWS, :] = (k == want - at).astype(jnp.float32).astype(jnp.bfloat16)


def advance(last, op_ref, x_ref, x_at, sel_ref, drive_ref, tau_ref, out_ref, new_ref):
    members = x_ref.shape[0]
    kblocks = drive_ref.shape[0]
    depth = members * ROWS

    def part(index):
        return x_ref[:, x_at + index * ROWS : x_at + (index + 1) * ROWS, :].reshape(depth, LANES)

    third = part(2)
    sums = [
        jnp.dot(
            op_ref[h * 256 : (h + 1) * 256, :],
            jnp.concatenate([part(h), third], axis=1),
            preferred_element_type=jnp.float32,
        )
        for h in range(2)
    ]
    both = sums[0][:, :LANES] + sums[1][:, :LANES]
    low = lax.broadcasted_iota(jnp.int32, (ROWS, LANES), 1) < HALF
    for r in range(kblocks):
        at = r * HALF
        pair = drive_ref[r, : 2 * ROWS, :] + tau_ref[r, : 2 * ROWS, :] * both[at : at + HALF]
        s00, s01 = (sums[0][at + h * ROWS : at + (h + 1) * ROWS, LANES:] for h in range(2))
        s10, s11 = (sums[1][at + h * ROWS : at + (h + 1) * ROWS, LANES:] for h in range(2))
        one = jnp.where(low, s00, s11) + turned(jnp.where(low, s01, s10))
        one = drive_ref[r, 2 * ROWS :, :] + tau_ref[r, 2 * ROWS :, :] * one
        if last:
            even, odd = pair[:ROWS], pair[ROWS:]
            new_ref[r, 0:ROWS, :] = jnp.where(low, even, turned(odd))
            new_ref[r, ROWS : 2 * ROWS, :] = jnp.where(low, turned(even), odd)
            new_ref[r, 2 * ROWS :, :] = one
        else:
            new_ref[r, : 2 * ROWS, :] = pair.astype(jnp.bfloat16)
            new_ref[r, 2 * ROWS :, :] = one.astype(jnp.bfloat16)
    if last:
        for k in range(kblocks):
            for c in range(BLOCK_ROWS):
                out_ref[k : k + 1, c * LANES : (c + 1) * LANES] = new_ref[k, c : c + 1, :]
    else:

        def block(d, carry):
            out_ref[d] = new_ref[sel_ref[d]]
            return carry

        lax.fori_loop(0, members, block, 0, unroll=8)


def first_kernel(sel_ref, x_ref, perm_ref, drive_ref, tau_ref, op_ref, out_ref, acc_ref, lab_ref, at_ref, pk_ref, sem):
    members = x_ref.shape[0]

    def read(s, carry):
        value = x_ref[s, LABEL_AT:FIRST_ROWS, :].astype(jnp.float32)
        lab_ref[pl.ds(s, 1), :] = (value[0:1] * 8.0 + value[1:2]).astype(jnp.int32)
        return carry

    lax.fori_loop(0, members, read, 0, unroll=8)
    copy = pltpu.make_async_copy(lab_ref, at_ref, sem)
    copy.start()
    acc_ref[...] = jnp.zeros_like(acc_ref)
    copy.wait()

    def add(s, carry):
        ats = [at_ref[s, c] for c in range(CAP)]
        tiles = [x_ref[s, c * ROWS : (c + 1) * ROWS, :].astype(jnp.float32) for c in range(CAP)]
        olds = [acc_ref[at] for at in ats]
        for c in range(CAP):
            value = olds[c] + tiles[c]
            for e in range(c):
                value = value + jnp.where(ats[e] == ats[c], tiles[e], 0.0)
            acc_ref[ats[c]] = value
        return carry

    lax.fori_loop(0, members, add, 0, unroll=2)

    groups = members // 4
    chunk = 8

    def turn(r, carry):
        for g0 in range(0, groups, chunk):
            parts = [[] for _ in range(4)]
            for g in range(g0, g0 + chunk):
                for q in range(4):
                    parts[q].append(acc_ref[r * members + g * 4 + q].astype(jnp.bfloat16))
            left = jnp.concatenate([jnp.concatenate(p, axis=0) for p in parts], axis=1)
            out = jnp.dot(left, perm_ref[...], preferred_element_type=jnp.float32).astype(jnp.bfloat16)
            for ha in range(2):
                for hb in range(2):
                    at = pl.multiple_of(hb * 256 + r * HALF + ha * ROWS, ROWS)
                    piece = out[:, (ha * 2 + hb) * LANES : (ha * 2 + hb + 1) * LANES]
                    for g in range(chunk):
                        op_ref[pl.ds(at, ROWS), (g0 + g) * LANES : (g0 + g + 1) * LANES] = piece[g * ROWS : (g + 1) * ROWS]
        return carry

    lax.fori_loop(0, 4, turn, 0)
    advance(False, op_ref, x_ref, TILE_ROWS, sel_ref, drive_ref, tau_ref, out_ref, pk_ref)


def step_kernel(last, sel_ref, x_ref, op_ref, drive_ref, tau_ref, out_ref, new_ref):
    advance(last, op_ref, x_ref, 0, sel_ref, drive_ref, tau_ref, out_ref, new_ref)


def shards(rates, tile_dest, tile_row, tile_col, send_list, drive, tau):
    members = lax.axis_size("pool") * lax.axis_size("ka")
    tiles = rates.shape[0]
    kblocks = drive.shape[0]
    exchange = functools.partial(lax.all_to_all, axis_name=AXES, split_axis=0, concat_axis=0, tiled=True)
    bf16, f32, i32 = jnp.bfloat16, jnp.float32, jnp.int32
    held = (kblocks, BLOCK_ROWS, LANES)
    sel = send_list.reshape(members)

    first, perm, drive_u, tau_u = pl.pallas_call(
        fill_kernel,
        out_shape=[
            jax.ShapeDtypeStruct((members, FIRST_ROWS, LANES), bf16),
            jax.ShapeDtypeStruct((4 * LANES, 4 * LANES), bf16),
            jax.ShapeDtypeStruct(held, f32),
            jax.ShapeDtypeStruct(held, f32),
        ],
        in_specs=[sspec()] * 4 + [vspec()] * 3,
        out_specs=[vspec()] * 4,
        scratch_shapes=[
            pltpu.SMEM((members,), i32),
            pltpu.VMEM((members, 1, LANES), i32),
            pltpu.VMEM(held, bf16),
            pltpu.VMEM((kblocks, BLOCK_ROWS + ROWS, LANES), f32),
        ],
        compiler_params=params(16),
        name="fill",
    )(tile_dest[:, 0], tile_row, tile_col, sel, rates.reshape(tiles, ROWS, LANES), drive, tau)
    first = exchange(first)

    operator, send = pl.pallas_call(
        first_kernel,
        out_shape=[
            jax.ShapeDtypeStruct((4 * LANES, members * ROWS), bf16),
            jax.ShapeDtypeStruct((members, BLOCK_ROWS, LANES), bf16),
        ],
        in_specs=[sspec()] + [vspec()] * 4,
        out_specs=[vspec()] * 2,
        scratch_shapes=[
            pltpu.VMEM((kblocks * members + 1, ROWS, LANES), f32),
            pltpu.VMEM((members, LANES), i32),
            pltpu.SMEM((members, LANES), i32),
            pltpu.VMEM(held, bf16),
            pltpu.SemaphoreType.DMA(()),
        ],
        compiler_params=params(32),
        name="first",
    )(sel, first, perm, drive_u, tau_u)

    for sweep in range(1, ITERS):
        last = sweep == ITERS - 1
        send = pl.pallas_call(
            functools.partial(step_kernel, last),
            out_shape=jax.ShapeDtypeStruct(drive.shape if last else send.shape, f32 if last else bf16),
            in_specs=[sspec()] + [vspec()] * 4,
            out_specs=vspec(),
            scratch_shapes=[pltpu.VMEM(held, f32 if last else bf16)],
            compiler_params=params(20),
            name="step_last" if last else "step",
        )(sel, exchange(send), operator, drive_u, tau_u)
    return send


def solution(mesh):
    pair = P(AXES, None)
    placed = (pair, pair, P(AXES), P(AXES), pair, pair, pair)
    return jax.shard_map(shards, mesh=mesh, in_specs=placed, out_specs=pair, check_vma=False)
```

```python
import functools

import jax
import jax.numpy as jnp
from jax import lax
from jax.experimental import pallas as pl
from jax.experimental.pallas import tpu as pltpu
from jax.sharding import PartitionSpec as P

ROWS = 32
LANES = 128
HALF = 64
ITERS = 3
CAP = 4
DIRS = 3
AXES = ("pool", "ka")
TILE_ROWS = CAP * ROWS
BLOCK_ROWS = DIRS * ROWS
LABEL_AT = TILE_ROWS + BLOCK_ROWS
FIRST_ROWS = LABEL_AT + 8

VMEM = pltpu.MemorySpace.VMEM
SMEM = pltpu.MemorySpace.SMEM


def vspec():
    return pl.BlockSpec(memory_space=VMEM)


def sspec():
    return pl.BlockSpec(memory_space=SMEM)


def params(mib):
    return pltpu.CompilerParams(vmem_limit_bytes=mib << 20)


def turned(value):
    return pltpu.roll(value, HALF, 1)


def low_half(rows):
    return lax.broadcasted_iota(jnp.int32, (rows, LANES), 1) < HALF


def send_block(k, even, odd, natural, rows_ref, pk_ref):
    low = low_half(ROWS)
    rows_ref[pl.ds(0, ROWS, stride=2), :] = even
    rows_ref[pl.ds(1, ROWS, stride=2), :] = odd
    pk_ref[k, :HALF, :] = rows_ref[...].astype(jnp.bfloat16)
    rows_ref[pl.ds(0, ROWS, stride=2), :] = natural
    rows_ref[pl.ds(1, ROWS, stride=2), :] = turned(natural)
    pk_ref[k, HALF:, :] = jnp.where(low, rows_ref[:ROWS, :], turned(rows_ref[ROWS:, :])).astype(jnp.bfloat16)


def fill_kernel(
    dest_ref, row_ref, col_ref, sel_ref, rates_ref, drive_ref, tau_ref, out_ref, du_ref, tu_ref, cnt_ref, lab_ref, pk_ref, nat_ref, rows_ref
):
    members = out_ref.shape[0]
    tiles = rates_ref.shape[0]
    kblocks = drive_ref.shape[0]
    lane = lax.broadcasted_iota(jnp.int32, (1, LANES), 1)
    low = low_half(ROWS)
    lab_ref[...] = jnp.full(lab_ref.shape, 4 * members, jnp.int32)

    for k in range(kblocks):
        for c in range(BLOCK_ROWS):
            nat_ref[k, c : c + 1, :] = drive_ref[k : k + 1, c * LANES : (c + 1) * LANES]
        for c in range(ROWS):
            nat_ref[k, BLOCK_ROWS + c : BLOCK_ROWS + c + 1, :] = tau_ref[k : k + 1, c * LANES : (c + 1) * LANES]
    for k in range(kblocks):
        n0, n1, n2, t = (nat_ref[k, n * ROWS : (n + 1) * ROWS, :] for n in range(DIRS + 1))
        even = jnp.where(low, n0, turned(n1))
        odd = jnp.where(low, turned(n0), n1)
        du_ref[k, 0:ROWS, :] = even
        du_ref[k, ROWS : 2 * ROWS, :] = odd
        du_ref[k, 2 * ROWS :, :] = n2
        tu_ref[k, 0:ROWS, :] = jnp.where(low, t, turned(t))
        tu_ref[k, ROWS : 2 * ROWS, :] = jnp.where(low, turned(t), t)
        tu_ref[k, 2 * ROWS :, :] = t
        send_block(k, even, odd, n2, rows_ref.at[k], pk_ref)

    def block(d, carry):
        cnt_ref[d] = 0
        out_ref[d, TILE_ROWS:LABEL_AT, :] = pk_ref[sel_ref[d]]
        return carry

    lax.fori_loop(0, members, block, 0, unroll=8)

    def place(i, carry):
        d = dest_ref[i]
        c = cnt_ref[d]
        cnt_ref[d] = c + 1
        where = row_ref[i] * members + col_ref[i]
        lab_ref[d] = jnp.where(lane == c, where, lab_ref[d])
        out_ref[d, pl.ds(pl.multiple_of(c * ROWS, ROWS), ROWS), :] = rates_ref[i]
        return carry

    lax.fori_loop(0, tiles, place, 0, unroll=4)

    sub = lax.broadcasted_iota(jnp.int32, (8, LANES), 0)

    def label(d, carry):
        value = jnp.broadcast_to(lab_ref[d], (8, LANES))
        value = jnp.where(sub == 0, value >> 3, value & 7)
        out_ref[d, LABEL_AT:FIRST_ROWS, :] = value.astype(jnp.float32).astype(jnp.bfloat16)
        return carry

    lax.fori_loop(0, members, label, 0, unroll=4)


def advance(last, op_ref, x_ref, x_at, sel_ref, drive_ref, tau_ref, out_ref, new_ref, rows_ref):
    members = x_ref.shape[0]
    kblocks = drive_ref.shape[0]
    low = low_half(ROWS)
    zero = jnp.zeros((), jnp.bfloat16)
    third = x_ref[:, x_at + HALF : x_at + BLOCK_ROWS, :]
    third = jnp.concatenate([jnp.where(low, third, zero), jnp.where(low, zero, third)], axis=1)
    pair = x_ref[:, x_at : x_at + HALF, :]
    right = jnp.concatenate([v.reshape(members * HALF, LANES) for v in (pair, third)], axis=1)
    total = jnp.dot(op_ref[...], right, preferred_element_type=jnp.float32)
    for r in range(kblocks):
        at = r * HALF
        pair = drive_ref[r, : 2 * ROWS, :] + tau_ref[r, : 2 * ROWS, :] * total[at : at + HALF, :LANES]
        even, odd = pair[:ROWS], pair[ROWS:]
        one = total[at : at + HALF, LANES:]
        one = one + turned(one)
        one = jnp.where(low, one[:ROWS], one[ROWS:])
        one = drive_ref[r, 2 * ROWS :, :] + tau_ref[r, 2 * ROWS :, :] * one
        if last:
            new_ref[r, 0:ROWS, :] = jnp.where(low, even, turned(odd))
            new_ref[r, ROWS : 2 * ROWS, :] = jnp.where(low, turned(even), odd)
            new_ref[r, 2 * ROWS :, :] = one
        else:
            send_block(r, even, odd, one, rows_ref.at[r], new_ref)
    if last:
        for k in range(kblocks):
            for c in range(BLOCK_ROWS):
                out_ref[k : k + 1, c * LANES : (c + 1) * LANES] = new_ref[k, c : c + 1, :]
    else:

        def block(d, carry):
            out_ref[d] = new_ref[sel_ref[d]]
            return carry

        lax.fori_loop(0, members, block, 0, unroll=8)


def first_kernel(sel_ref, x_ref, drive_ref, tau_ref, op_ref, out_ref, acc_ref, lab_ref, at_ref, pk_ref, rows_ref, sem):
    members = x_ref.shape[0]
    kblocks = drive_ref.shape[0]

    def read(s, carry):
        value = x_ref[s, LABEL_AT:FIRST_ROWS, :].astype(jnp.float32)
        lab_ref[pl.ds(s, 1), :] = (value[0:1] * 8.0 + value[1:2]).astype(jnp.int32)
        return carry

    lax.fori_loop(0, members, read, 0, unroll=8)
    copy = pltpu.make_async_copy(lab_ref, at_ref, sem)
    copy.start()
    acc_ref[...] = jnp.zeros_like(acc_ref)
    copy.wait()

    def add(s, carry):
        ats = [at_ref[s, c] for c in range(CAP)]
        olds = [acc_ref[at] for at in ats]
        news = []
        for c in range(CAP):
            old = olds[c]
            for e in range(c):
                old = jnp.where(ats[e] == ats[c], news[e], old)
            news.append(old + x_ref[s, c * ROWS : (c + 1) * ROWS, :].astype(jnp.float32))
        for c in range(CAP):
            acc_ref[ats[c]] = news[c]
        return carry

    lax.fori_loop(0, members, add, 0, unroll=2)

    low = low_half(ROWS)

    def join(r, carry):
        at = pl.multiple_of(r * HALF, HALF)
        for g in range(members // 2):
            a = acc_ref[r * members + 2 * g]
            b = acc_ref[r * members + 2 * g + 1]
            lanes = slice(g * LANES, (g + 1) * LANES)
            op_ref[pl.ds(at, ROWS), lanes] = jnp.where(low, a, turned(b)).astype(jnp.bfloat16)
            op_ref[pl.ds(at + ROWS, ROWS), lanes] = jnp.where(low, turned(a), b).astype(jnp.bfloat16)
        return carry

    lax.fori_loop(0, kblocks, join, 0)
    advance(False, op_ref, x_ref, TILE_ROWS, sel_ref, drive_ref, tau_ref, out_ref, pk_ref, rows_ref)


def step_kernel(last, sel_ref, x_ref, op_ref, drive_ref, tau_ref, out_ref, new_ref, rows_ref):
    advance(last, op_ref, x_ref, 0, sel_ref, drive_ref, tau_ref, out_ref, new_ref, rows_ref)


def shards(rates, tile_dest, tile_row, tile_col, send_list, drive, tau):
    members = lax.axis_size("pool") * lax.axis_size("ka")
    tiles = rates.shape[0]
    kblocks = drive.shape[0]
    exchange = functools.partial(lax.all_to_all, axis_name=AXES, split_axis=0, concat_axis=0, tiled=True)
    bf16, f32, i32 = jnp.bfloat16, jnp.float32, jnp.int32
    held = (kblocks, BLOCK_ROWS, LANES)
    rows = pltpu.VMEM((kblocks, HALF, LANES), f32)
    sel = send_list.reshape(members)

    first, drive_u, tau_u = pl.pallas_call(
        fill_kernel,
        out_shape=[
            jax.ShapeDtypeStruct((members, FIRST_ROWS, LANES), bf16),
            jax.ShapeDtypeStruct(held, f32),
            jax.ShapeDtypeStruct(held, f32),
        ],
        in_specs=[sspec()] * 4 + [vspec()] * 3,
        out_specs=[vspec()] * 3,
        scratch_shapes=[
            pltpu.SMEM((members,), i32),
            pltpu.VMEM((members, 1, LANES), i32),
            pltpu.VMEM(held, bf16),
            pltpu.VMEM((kblocks, BLOCK_ROWS + ROWS, LANES), f32),
            rows,
        ],
        compiler_params=params(16),
        name="fill",
    )(tile_dest[:, 0], tile_row, tile_col, sel, rates.reshape(tiles, ROWS, LANES), drive, tau)
    first = exchange(first)

    operator, send = pl.pallas_call(
        first_kernel,
        out_shape=[
            jax.ShapeDtypeStruct((kblocks * HALF, members * HALF), bf16),
            jax.ShapeDtypeStruct((members, BLOCK_ROWS, LANES), bf16),
        ],
        in_specs=[sspec()] + [vspec()] * 3,
        out_specs=[vspec()] * 2,
        scratch_shapes=[
            pltpu.VMEM((kblocks * members + 1, ROWS, LANES), f32),
            pltpu.VMEM((members, LANES), i32),
            pltpu.SMEM((members, LANES), i32),
            pltpu.VMEM(held, bf16),
            rows,
            pltpu.SemaphoreType.DMA(()),
        ],
        compiler_params=params(32),
        name="first",
    )(sel, first, drive_u, tau_u)

    for sweep in range(1, ITERS):
        last = sweep == ITERS - 1
        send = pl.pallas_call(
            functools.partial(step_kernel, last),
            out_shape=jax.ShapeDtypeStruct(drive.shape if last else send.shape, f32 if last else bf16),
            in_specs=[sspec()] + [vspec()] * 4,
            out_specs=vspec(),
            scratch_shapes=[pltpu.VMEM(held, f32 if last else bf16), rows],
            compiler_params=params(20),
            name="step_last" if last else "step",
        )(sel, exchange(send), operator, drive_u, tau_u)
    return send


def solution(mesh):
    pair = P(AXES, None)
    placed = (pair, pair, P(AXES), P(AXES), pair, pair, pair)
    return jax.shard_map(shards, mesh=mesh, in_specs=placed, out_specs=pair, check_vma=False)
```

```python
import functools

import jax
import jax.numpy as jnp
from jax import lax
from jax.experimental import pallas as pl
from jax.experimental.pallas import tpu as pltpu
from jax.sharding import PartitionSpec as P

ROWS = 32
LANES = 128
HALF = 64
ITERS = 3
CAP = 4
DIRS = 3
AXES = ("pool", "ka")
TILE_ROWS = CAP * ROWS
BLOCK_ROWS = DIRS * ROWS
LABEL_AT = TILE_ROWS + BLOCK_ROWS
FIRST_ROWS = LABEL_AT + 8

VMEM = pltpu.MemorySpace.VMEM
SMEM = pltpu.MemorySpace.SMEM


def vspec():
    return pl.BlockSpec(memory_space=VMEM)


def sspec():
    return pl.BlockSpec(memory_space=SMEM)


def params(mib):
    return pltpu.CompilerParams(vmem_limit_bytes=mib << 20)


def turned(value):
    return pltpu.roll(value, HALF, 1)


def low_half(rows):
    return lax.broadcasted_iota(jnp.int32, (rows, LANES), 1) < HALF


def send_block(k, even, odd, natural, rows_ref, pk_ref):
    low = low_half(ROWS)
    rows_ref[pl.ds(0, ROWS, stride=2), :] = even
    rows_ref[pl.ds(1, ROWS, stride=2), :] = odd
    pk_ref[k, :HALF, :] = rows_ref[...].astype(jnp.bfloat16)
    rows_ref[pl.ds(0, ROWS, stride=2), :] = natural
    rows_ref[pl.ds(1, ROWS, stride=2), :] = turned(natural)
    pk_ref[k, HALF:, :] = jnp.where(low, rows_ref[:ROWS, :], turned(rows_ref[ROWS:, :])).astype(jnp.bfloat16)


def fill_kernel(
    dest_ref, sel_ref, dests_ref, tile_rows_ref, cols_ref, rates_ref, drive_ref, tau_ref, out_ref, du_ref, tu_ref,
    slot_ref, slots_ref, lab_ref, pk_ref, nat_ref, rows_ref, sem,
):
    members = out_ref.shape[0]
    tiles = rates_ref.shape[0]
    kblocks = drive_ref.shape[0]
    f32, bf16, i32 = jnp.float32, jnp.bfloat16, jnp.int32
    low = low_half(ROWS)

    named = (lax.broadcasted_iota(i32, (members, tiles), 0) == dests_ref[...]).astype(f32)
    i0 = lax.broadcasted_iota(i32, (tiles, tiles), 0)
    i1 = lax.broadcasted_iota(i32, (tiles, tiles), 1)
    earlier = jnp.dot(named.astype(bf16), (i0 < i1).astype(f32).astype(bf16), preferred_element_type=f32)
    slot = jnp.sum(named * earlier, axis=0, keepdims=True).astype(i32)
    slot_ref[...] = slot
    copy = pltpu.make_async_copy(slot_ref, slots_ref, sem)
    copy.start()
    where = tile_rows_ref[...] * members + cols_ref[...]
    sub = lax.broadcasted_iota(i32, (LANES, tiles), 0)
    value = jnp.where(sub < CAP, (where >> 3) - 4 * members // 8, where & 7)
    value = jnp.where((slot == (sub & (CAP - 1))) & (sub < 2 * CAP), value, 0)
    lab_ref[...] = lax.dot_general(
        named.astype(bf16), value.astype(f32).astype(bf16), (((1,), (1,)), ((), ())), preferred_element_type=f32
    )

    for k in range(kblocks):
        for c in range(BLOCK_ROWS):
            nat_ref[k, c : c + 1, :] = drive_ref[k : k + 1, c * LANES : (c + 1) * LANES]
        for c in range(ROWS):
            nat_ref[k, BLOCK_ROWS + c : BLOCK_ROWS + c + 1, :] = tau_ref[k : k + 1, c * LANES : (c + 1) * LANES]
    for k in range(kblocks):
        n0, n1, n2, t = (nat_ref[k, n * ROWS : (n + 1) * ROWS, :] for n in range(DIRS + 1))
        even = jnp.where(low, n0, turned(n1))
        odd = jnp.where(low, turned(n0), n1)
        du_ref[k, 0:ROWS, :] = even
        du_ref[k, ROWS : 2 * ROWS, :] = odd
        du_ref[k, 2 * ROWS :, :] = n2
        tu_ref[k, 0:ROWS, :] = jnp.where(low, t, turned(t))
        tu_ref[k, ROWS : 2 * ROWS, :] = jnp.where(low, turned(t), t)
        tu_ref[k, 2 * ROWS :, :] = t
        send_block(k, even, odd, n2, rows_ref.at[k], pk_ref)

    def block(d, carry):
        out_ref[d, TILE_ROWS:LABEL_AT, :] = pk_ref[sel_ref[d]]
        out_ref[d, LABEL_AT:FIRST_ROWS, :] = jnp.broadcast_to(lab_ref[pl.ds(d, 1), :], (8, LANES)).astype(bf16)
        return carry

    lax.fori_loop(0, members, block, 0, unroll=8)
    copy.wait()

    def move(i, carry):
        start = pl.multiple_of(slots_ref[0, i] * ROWS, ROWS)
        out_ref[dest_ref[i], pl.ds(start, ROWS), :] = rates_ref[i]
        return carry

    lax.fori_loop(0, tiles, move, 0, unroll=8)


def advance(last, op_ref, x_ref, x_at, sel_ref, drive_ref, tau_ref, out_ref, new_ref, rows_ref):
    members = x_ref.shape[0]
    kblocks = drive_ref.shape[0]
    low = low_half(ROWS)
    zero = jnp.zeros((), jnp.bfloat16)
    third = x_ref[:, x_at + HALF : x_at + BLOCK_ROWS, :]
    third = jnp.concatenate([jnp.where(low, third, zero), jnp.where(low, zero, third)], axis=1)
    pair = x_ref[:, x_at : x_at + HALF, :]
    right = jnp.concatenate([v.reshape(members * HALF, LANES) for v in (pair, third)], axis=1)
    total = jnp.dot(op_ref[...], right, preferred_element_type=jnp.float32)
    for r in range(kblocks):
        at = r * HALF
        pair = drive_ref[r, : 2 * ROWS, :] + tau_ref[r, : 2 * ROWS, :] * total[at : at + HALF, :LANES]
        even, odd = pair[:ROWS], pair[ROWS:]
        one = total[at : at + HALF, LANES:]
        one = one + turned(one)
        one = jnp.where(low, one[:ROWS], one[ROWS:])
        one = drive_ref[r, 2 * ROWS :, :] + tau_ref[r, 2 * ROWS :, :] * one
        if last:
            new_ref[r, 0:ROWS, :] = jnp.where(low, even, turned(odd))
            new_ref[r, ROWS : 2 * ROWS, :] = jnp.where(low, turned(even), odd)
            new_ref[r, 2 * ROWS :, :] = one
        else:
            send_block(r, even, odd, one, rows_ref.at[r], new_ref)
    if last:
        for k in range(kblocks):
            for c in range(BLOCK_ROWS):
                out_ref[k : k + 1, c * LANES : (c + 1) * LANES] = new_ref[k, c : c + 1, :]
    else:

        def block(d, carry):
            out_ref[d] = new_ref[sel_ref[d]]
            return carry

        lax.fori_loop(0, members, block, 0, unroll=8)


def first_kernel(sel_ref, x_ref, drive_ref, tau_ref, op_ref, out_ref, acc_ref, raw_ref, lab_ref, at_ref, pk_ref, rows_ref, sem):
    members = x_ref.shape[0]
    kblocks = drive_ref.shape[0]

    none = 4 * members

    def read(s, carry):
        raw_ref[pl.ds(s, 1), :] = x_ref[s, LABEL_AT:FIRST_ROWS, :].astype(jnp.float32)[0:1]
        return carry

    lax.fori_loop(0, members, read, 0, unroll=8)
    raw = raw_ref[...]
    place = (raw * 8.0 + pltpu.roll(raw, LANES - CAP, 1)).astype(jnp.int32) + none
    lane = lax.broadcasted_iota(jnp.int32, place.shape, 1)
    lost = jnp.zeros_like(place)
    for k in range(1, CAP):
        again = (place == pltpu.roll(place, LANES - k, 1)) & (lane < CAP - k) & (place < none)
        lost = jnp.where(again, 1, lost)
    some = lost
    for k in range(1, CAP):
        some = some + pltpu.roll(lost, k, 1)
    place = jnp.where(lane < CAP, place, jnp.where(lane < 2 * CAP, pltpu.roll(lost, CAP, 1), pltpu.roll(some, CAP + 1, 1)))
    lab_ref[...] = place
    copy = pltpu.make_async_copy(lab_ref, at_ref, sem)
    copy.start()
    acc_ref[...] = jnp.zeros_like(acc_ref)
    copy.wait()

    def tile(s, c):
        return x_ref[s, c * ROWS : (c + 1) * ROWS, :].astype(jnp.float32)

    def repair(s):
        for c in range(CAP - 1):

            @pl.when(at_ref[s, CAP + c] > 0)
            def _():
                at = at_ref[s, c]
                acc_ref[at] = acc_ref[at] + tile(s, c)

    def add(h, carry):
        for s in (2 * h, 2 * h + 1):
            ats = [at_ref[s, c] for c in range(CAP)]
            news = [acc_ref[ats[c]] + tile(s, c) for c in range(CAP)]
            for c in range(CAP):
                acc_ref[ats[c]] = news[c]

        @pl.when(at_ref[2 * h, 2 * CAP] + at_ref[2 * h + 1, 2 * CAP] > 0)
        def _():
            repair(2 * h)
            repair(2 * h + 1)

        return carry

    lax.fori_loop(0, members // 2, add, 0)

    low = low_half(ROWS)

    def join(r, carry):
        at = pl.multiple_of(r * HALF, HALF)
        for g in range(members // 2):
            a = acc_ref[r * members + 2 * g]
            b = acc_ref[r * members + 2 * g + 1]
            lanes = slice(g * LANES, (g + 1) * LANES)
            swap = turned(jnp.where(low, b, a))
            op_ref[pl.ds(at, ROWS), lanes] = jnp.where(low, a, swap).astype(jnp.bfloat16)
            op_ref[pl.ds(at + ROWS, ROWS), lanes] = jnp.where(low, swap, b).astype(jnp.bfloat16)
        return carry

    lax.fori_loop(0, kblocks, join, 0)
    advance(False, op_ref, x_ref, TILE_ROWS, sel_ref, drive_ref, tau_ref, out_ref, pk_ref, rows_ref)


def step_kernel(last, sel_ref, x_ref, op_ref, drive_ref, tau_ref, out_ref, new_ref, rows_ref):
    advance(last, op_ref, x_ref, 0, sel_ref, drive_ref, tau_ref, out_ref, new_ref, rows_ref)


def shards(rates, tile_dest, tile_row, tile_col, send_list, drive, tau):
    members = lax.axis_size("pool") * lax.axis_size("ka")
    tiles = rates.shape[0]
    kblocks = drive.shape[0]
    exchange = functools.partial(lax.all_to_all, axis_name=AXES, split_axis=0, concat_axis=0, tiled=True)
    bf16, f32, i32 = jnp.bfloat16, jnp.float32, jnp.int32
    held = (kblocks, BLOCK_ROWS, LANES)
    rows = pltpu.VMEM((kblocks, HALF, LANES), f32)
    sel = send_list.reshape(members)

    first, drive_u, tau_u = pl.pallas_call(
        fill_kernel,
        out_shape=[
            jax.ShapeDtypeStruct((members, FIRST_ROWS, LANES), bf16),
            jax.ShapeDtypeStruct(held, f32),
            jax.ShapeDtypeStruct(held, f32),
        ],
        in_specs=[sspec()] * 2 + [vspec()] * 6,
        out_specs=[vspec()] * 3,
        scratch_shapes=[
            pltpu.VMEM((1, tiles), i32),
            pltpu.SMEM((1, tiles), i32),
            pltpu.VMEM((members, LANES), f32),
            pltpu.VMEM(held, bf16),
            pltpu.VMEM((kblocks, BLOCK_ROWS + ROWS, LANES), f32),
            rows,
            pltpu.SemaphoreType.DMA(()),
        ],
        compiler_params=params(16),
        name="fill",
    )(
        tile_dest[:, 0],
        sel,
        tile_dest.reshape(1, tiles),
        tile_row.reshape(1, tiles),
        tile_col.reshape(1, tiles),
        rates.reshape(tiles, ROWS, LANES),
        drive,
        tau,
    )
    first = exchange(first)

    operator, send = pl.pallas_call(
        first_kernel,
        out_shape=[
            jax.ShapeDtypeStruct((kblocks * HALF, members * HALF), bf16),
            jax.ShapeDtypeStruct((members, BLOCK_ROWS, LANES), bf16),
        ],
        in_specs=[sspec()] + [vspec()] * 3,
        out_specs=[vspec()] * 2,
        scratch_shapes=[
            pltpu.VMEM((kblocks * members + 1, ROWS, LANES), f32),
            pltpu.VMEM((members, LANES), f32),
            pltpu.VMEM((members, LANES), i32),
            pltpu.SMEM((members, LANES), i32),
            pltpu.VMEM(held, bf16),
            rows,
            pltpu.SemaphoreType.DMA(()),
        ],
        compiler_params=params(32),
        name="first",
    )(sel, first, drive_u, tau_u)

    for sweep in range(1, ITERS):
        last = sweep == ITERS - 1
        send = pl.pallas_call(
            functools.partial(step_kernel, last),
            out_shape=jax.ShapeDtypeStruct(drive.shape if last else send.shape, f32 if last else bf16),
            in_specs=[sspec()] + [vspec()] * 4,
            out_specs=vspec(),
            scratch_shapes=[pltpu.VMEM(held, f32 if last else bf16), rows],
            compiler_params=params(20),
            name="step_last" if last else "step",
        )(sel, exchange(send), operator, drive_u, tau_u)
    return send


def solution(mesh):
    pair = P(AXES, None)
    placed = (pair, pair, P(AXES), P(AXES), pair, pair, pair)
    return jax.shard_map(shards, mesh=mesh, in_specs=placed, out_specs=pair, check_vma=False)
```

```python
import functools

import jax
import jax.numpy as jnp
from jax import lax
from jax.experimental import pallas as pl
from jax.experimental.pallas import tpu as pltpu
from jax.sharding import PartitionSpec as P

ROWS = 32
LANES = 128
HALF = 64
ITERS = 3
CAP = 4
DIRS = 3
AXES = ("pool", "ka")
TILE_ROWS = CAP * ROWS
BLOCK_ROWS = DIRS * ROWS
LABEL_AT = TILE_ROWS + BLOCK_ROWS
FIRST_ROWS = LABEL_AT + 8

VMEM = pltpu.MemorySpace.VMEM
SMEM = pltpu.MemorySpace.SMEM


def vspec():
    return pl.BlockSpec(memory_space=VMEM)


def sspec():
    return pl.BlockSpec(memory_space=SMEM)


def params(mib):
    return pltpu.CompilerParams(vmem_limit_bytes=mib << 20)


def turned(value):
    return pltpu.roll(value, HALF, 1)


def low_half(rows):
    return lax.broadcasted_iota(jnp.int32, (rows, LANES), 1) < HALF


def send_block(k, even, odd, natural, rows_ref, pk_ref):
    low = low_half(ROWS)
    rows_ref[pl.ds(0, ROWS, stride=2), :] = even
    rows_ref[pl.ds(1, ROWS, stride=2), :] = odd
    pk_ref[k, :HALF, :] = rows_ref[...].astype(jnp.bfloat16)
    rows_ref[pl.ds(0, ROWS, stride=2), :] = natural
    rows_ref[pl.ds(1, ROWS, stride=2), :] = turned(natural)
    pk_ref[k, HALF:, :] = jnp.where(low, rows_ref[:ROWS, :], turned(rows_ref[ROWS:, :])).astype(jnp.bfloat16)


def fill_kernel(
    dest_ref, sel_ref, dests_ref, tile_rows_ref, cols_ref, rates_ref, drive_ref, tau_ref, out_ref, du_ref, tu_ref,
    slot_ref, slots_ref, lab_ref, pk_ref, nat_ref, rows_ref, sem,
):
    members = out_ref.shape[0]
    tiles = rates_ref.shape[0]
    kblocks = drive_ref.shape[0]
    f32, bf16, i32 = jnp.float32, jnp.bfloat16, jnp.int32
    low = low_half(ROWS)

    named = (lax.broadcasted_iota(i32, (members, tiles), 0) == dests_ref[...]).astype(f32)
    i0 = lax.broadcasted_iota(i32, (tiles, tiles), 0)
    i1 = lax.broadcasted_iota(i32, (tiles, tiles), 1)
    earlier = jnp.dot(named.astype(bf16), (i0 < i1).astype(f32).astype(bf16), preferred_element_type=f32)
    slot = jnp.sum(named * earlier, axis=0, keepdims=True).astype(i32)
    slot_ref[...] = slot
    copy = pltpu.make_async_copy(slot_ref, slots_ref, sem)
    copy.start()
    where = tile_rows_ref[...] * members + cols_ref[...]
    sub = lax.broadcasted_iota(i32, (LANES, tiles), 0)
    value = jnp.where(sub < CAP, (where >> 3) - 4 * members // 8, where & 7)
    value = jnp.where((slot == (sub & (CAP - 1))) & (sub < 2 * CAP), value, 0)
    lab_ref[...] = lax.dot_general(
        named.astype(bf16), value.astype(f32).astype(bf16), (((1,), (1,)), ((), ())), preferred_element_type=f32
    )

    for k in range(kblocks):
        for c in range(BLOCK_ROWS):
            nat_ref[k, c : c + 1, :] = drive_ref[k : k + 1, c * LANES : (c + 1) * LANES]
        for c in range(ROWS):
            nat_ref[k, BLOCK_ROWS + c : BLOCK_ROWS + c + 1, :] = tau_ref[k : k + 1, c * LANES : (c + 1) * LANES]
    for k in range(kblocks):
        n0, n1, n2, t = (nat_ref[k, n * ROWS : (n + 1) * ROWS, :] for n in range(DIRS + 1))
        even = jnp.where(low, n0, turned(n1))
        odd = jnp.where(low, turned(n0), n1)
        du_ref[k, 0:ROWS, :] = even
        du_ref[k, ROWS : 2 * ROWS, :] = odd
        du_ref[k, 2 * ROWS :, :] = n2
        tu_ref[k, 0:ROWS, :] = jnp.where(low, t, turned(t))
        tu_ref[k, ROWS : 2 * ROWS, :] = jnp.where(low, turned(t), t)
        tu_ref[k, 2 * ROWS :, :] = t
        send_block(k, even, odd, n2, rows_ref.at[k], pk_ref)

    def block(d, carry):
        out_ref[d, TILE_ROWS:LABEL_AT, :] = pk_ref[sel_ref[d]]
        out_ref[d, LABEL_AT:FIRST_ROWS, :] = jnp.broadcast_to(lab_ref[pl.ds(d, 1), :], (8, LANES)).astype(bf16)
        return carry

    lax.fori_loop(0, members, block, 0, unroll=8)
    copy.wait()

    def move(i, carry):
        start = pl.multiple_of(slots_ref[0, i] * ROWS, ROWS)
        out_ref[dest_ref[i], pl.ds(start, ROWS), :] = rates_ref[i]
        return carry

    lax.fori_loop(0, tiles, move, 0, unroll=8)


def advance(last, op_ref, x_ref, x_at, sel_ref, drive_ref, tau_ref, out_ref, new_ref, rows_ref, prepare=None, chunks=1):
    members = x_ref.shape[0]
    kblocks = drive_ref.shape[0]
    low = low_half(ROWS)
    zero = jnp.zeros((), jnp.bfloat16)
    some = members // chunks
    total = None
    for q in range(chunks):
        if prepare is not None:
            prepare(q)
        entries = slice(q * some, (q + 1) * some)
        third = x_ref[entries, x_at + HALF : x_at + BLOCK_ROWS, :]
        third = jnp.concatenate([jnp.where(low, third, zero), jnp.where(low, zero, third)], axis=1)
        pair = x_ref[entries, x_at : x_at + HALF, :]
        right = jnp.concatenate([v.reshape(some * HALF, LANES) for v in (pair, third)], axis=1)
        left = op_ref[:, q * some * HALF : (q + 1) * some * HALF]
        part = jnp.dot(left, right, preferred_element_type=jnp.float32)
        total = part if total is None else total + part
    for r in range(kblocks):
        at = r * HALF
        pair = drive_ref[r, : 2 * ROWS, :] + tau_ref[r, : 2 * ROWS, :] * total[at : at + HALF, :LANES]
        even, odd = pair[:ROWS], pair[ROWS:]
        one = total[at : at + HALF, LANES:]
        one = one + turned(one)
        one = jnp.where(low, one[:ROWS], one[ROWS:])
        one = drive_ref[r, 2 * ROWS :, :] + tau_ref[r, 2 * ROWS :, :] * one
        if last:
            new_ref[r, 0:ROWS, :] = jnp.where(low, even, turned(odd))
            new_ref[r, ROWS : 2 * ROWS, :] = jnp.where(low, turned(even), odd)
            new_ref[r, 2 * ROWS :, :] = one
        else:
            send_block(r, even, odd, one, rows_ref.at[r], new_ref)
    if last:
        for k in range(kblocks):
            for c in range(BLOCK_ROWS):
                out_ref[k : k + 1, c * LANES : (c + 1) * LANES] = new_ref[k, c : c + 1, :]
    else:

        def block(d, carry):
            out_ref[d] = new_ref[sel_ref[d]]
            return carry

        lax.fori_loop(0, members, block, 0, unroll=8)


def first_kernel(sel_ref, x_ref, drive_ref, tau_ref, op_ref, out_ref, acc_ref, raw_ref, lab_ref, at_ref, pk_ref, rows_ref, sem):
    members = x_ref.shape[0]
    kblocks = drive_ref.shape[0]

    none = 4 * members

    def read(s, carry):
        raw_ref[pl.ds(s, 1), :] = x_ref[s, LABEL_AT:FIRST_ROWS, :].astype(jnp.float32)[0:1]
        return carry

    lax.fori_loop(0, members, read, 0, unroll=8)
    raw = raw_ref[...]
    place = (raw * 8.0 + pltpu.roll(raw, LANES - CAP, 1)).astype(jnp.int32) + none
    lab_ref[...] = place
    copy = pltpu.make_async_copy(lab_ref, at_ref, sem)
    copy.start()
    acc_ref[...] = jnp.zeros_like(acc_ref)
    copy.wait()

    def add(s, carry):
        ats = [at_ref[s, c] for c in range(CAP)]
        olds = [acc_ref[at] for at in ats]
        sums = []
        for c in range(CAP):
            same = jnp.zeros((ROWS, LANES), jnp.float32)
            for e in range(c):
                same = jnp.where(ats[e] == ats[c], sums[e], same)
            tile = x_ref[s, c * ROWS : (c + 1) * ROWS, :].astype(jnp.float32)
            sums.append(tile + same if c else tile)
        for c in range(CAP):
            acc_ref[ats[c]] = olds[c] + sums[c]
        return carry

    lax.fori_loop(0, members, add, 0, unroll=4)

    low = low_half(ROWS)

    pairs = members // 2 // 16

    def join(q):
        for g in range(q * pairs, (q + 1) * pairs):
            for r in range(kblocks):
                at = r * HALF
                a = acc_ref[r * members + 2 * g]
                b = acc_ref[r * members + 2 * g + 1]
                lanes = slice(g * LANES, (g + 1) * LANES)
                swap = turned(jnp.where(low, b, a))
                op_ref[at : at + ROWS, lanes] = jnp.where(low, a, swap).astype(jnp.bfloat16)
                op_ref[at + ROWS : at + HALF, lanes] = jnp.where(low, swap, b).astype(jnp.bfloat16)

    advance(False, op_ref, x_ref, TILE_ROWS, sel_ref, drive_ref, tau_ref, out_ref, pk_ref, rows_ref, join, 16)


def step_kernel(last, sel_ref, x_ref, op_ref, drive_ref, tau_ref, out_ref, new_ref, rows_ref):
    advance(last, op_ref, x_ref, 0, sel_ref, drive_ref, tau_ref, out_ref, new_ref, rows_ref)


def shards(rates, tile_dest, tile_row, tile_col, send_list, drive, tau):
    members = lax.axis_size("pool") * lax.axis_size("ka")
    tiles = rates.shape[0]
    kblocks = drive.shape[0]
    exchange = functools.partial(lax.all_to_all, axis_name=AXES, split_axis=0, concat_axis=0, tiled=True)
    bf16, f32, i32 = jnp.bfloat16, jnp.float32, jnp.int32
    held = (kblocks, BLOCK_ROWS, LANES)
    rows = pltpu.VMEM((kblocks, HALF, LANES), f32)
    sel = send_list.reshape(members)

    first, drive_u, tau_u = pl.pallas_call(
        fill_kernel,
        out_shape=[
            jax.ShapeDtypeStruct((members, FIRST_ROWS, LANES), bf16),
            jax.ShapeDtypeStruct(held, f32),
            jax.ShapeDtypeStruct(held, f32),
        ],
        in_specs=[sspec()] * 2 + [vspec()] * 6,
        out_specs=[vspec()] * 3,
        scratch_shapes=[
            pltpu.VMEM((1, tiles), i32),
            pltpu.SMEM((1, tiles), i32),
            pltpu.VMEM((members, LANES), f32),
            pltpu.VMEM(held, bf16),
            pltpu.VMEM((kblocks, BLOCK_ROWS + ROWS, LANES), f32),
            rows,
            pltpu.SemaphoreType.DMA(()),
        ],
        compiler_params=params(16),
        name="fill",
    )(
        tile_dest[:, 0],
        sel,
        tile_dest.reshape(1, tiles),
        tile_row.reshape(1, tiles),
        tile_col.reshape(1, tiles),
        rates.reshape(tiles, ROWS, LANES),
        drive,
        tau,
    )
    first = exchange(first)

    operator, send = pl.pallas_call(
        first_kernel,
        out_shape=[
            jax.ShapeDtypeStruct((kblocks * HALF, members * HALF), bf16),
            jax.ShapeDtypeStruct((members, BLOCK_ROWS, LANES), bf16),
        ],
        in_specs=[sspec()] + [vspec()] * 3,
        out_specs=[vspec()] * 2,
        scratch_shapes=[
            pltpu.VMEM((kblocks * members + 1, ROWS, LANES), f32),
            pltpu.VMEM((members, LANES), f32),
            pltpu.VMEM((members, LANES), i32),
            pltpu.SMEM((members, LANES), i32),
            pltpu.VMEM(held, bf16),
            rows,
            pltpu.SemaphoreType.DMA(()),
        ],
        compiler_params=params(32),
        name="first",
    )(sel, first, drive_u, tau_u)

    for sweep in range(1, ITERS):
        last = sweep == ITERS - 1
        send = pl.pallas_call(
            functools.partial(step_kernel, last),
            out_shape=jax.ShapeDtypeStruct(drive.shape if last else send.shape, f32 if last else bf16),
            in_specs=[sspec()] + [vspec()] * 4,
            out_specs=vspec(),
            scratch_shapes=[pltpu.VMEM(held, f32 if last else bf16), rows],
            compiler_params=params(20),
            name="step_last" if last else "step",
        )(sel, exchange(send), operator, drive_u, tau_u)
    return send


def solution(mesh):
    pair = P(AXES, None)
    placed = (pair, pair, P(AXES), P(AXES), pair, pair, pair)
    return jax.shard_map(shards, mesh=mesh, in_specs=placed, out_specs=pair, check_vma=False)
```

```python
import functools

import jax
import jax.numpy as jnp
from jax import lax
from jax.experimental import pallas as pl
from jax.experimental.pallas import tpu as pltpu
from jax.sharding import PartitionSpec as P

ROWS = 32
LANES = 128
HALF = 64
ITERS = 3
CAP = 4
DIRS = 3
AXES = ("pool", "ka")
TILE_ROWS = CAP * ROWS
BLOCK_ROWS = DIRS * ROWS
LABEL_AT = TILE_ROWS + BLOCK_ROWS
FIRST_ROWS = LABEL_AT + 8

VMEM = pltpu.MemorySpace.VMEM
SMEM = pltpu.MemorySpace.SMEM


def vspec():
    return pl.BlockSpec(memory_space=VMEM)


def sspec():
    return pl.BlockSpec(memory_space=SMEM)


def params(mib):
    return pltpu.CompilerParams(vmem_limit_bytes=mib << 20)


def turned(value):
    return pltpu.roll(value, HALF, 1)


def low_half(rows):
    return lax.broadcasted_iota(jnp.int32, (rows, LANES), 1) < HALF


def send_block(k, even, odd, natural, rows_ref, pk_ref):
    low = low_half(ROWS)
    rows_ref[pl.ds(0, ROWS, stride=2), :] = even
    rows_ref[pl.ds(1, ROWS, stride=2), :] = odd
    pk_ref[k, :HALF, :] = rows_ref[...].astype(jnp.bfloat16)
    rows_ref[pl.ds(0, ROWS, stride=2), :] = natural
    rows_ref[pl.ds(1, ROWS, stride=2), :] = turned(natural)
    pk_ref[k, HALF:, :] = jnp.where(low, rows_ref[:ROWS, :], turned(rows_ref[ROWS:, :])).astype(jnp.bfloat16)


def fill_kernel(
    dest_ref, sel_ref, dests_ref, tile_rows_ref, cols_ref, rates_ref, drive_ref, tau_ref, out_ref, du_ref, tu_ref,
    slot_ref, slots_ref, lab_ref, pk_ref, nat_ref, rows_ref, sem,
):
    members = out_ref.shape[0]
    tiles = rates_ref.shape[0]
    kblocks = drive_ref.shape[0]
    f32, bf16, i32 = jnp.float32, jnp.bfloat16, jnp.int32
    low = low_half(ROWS)

    named = (lax.broadcasted_iota(i32, (members, tiles), 0) == dests_ref[...]).astype(f32)
    i0 = lax.broadcasted_iota(i32, (tiles, tiles), 0)
    i1 = lax.broadcasted_iota(i32, (tiles, tiles), 1)
    earlier = jnp.dot(named.astype(bf16), (i0 < i1).astype(f32).astype(bf16), preferred_element_type=f32)
    slot = jnp.sum(named * earlier, axis=0, keepdims=True).astype(i32)
    slot_ref[...] = slot
    copy = pltpu.make_async_copy(slot_ref, slots_ref, sem)
    copy.start()
    where = tile_rows_ref[...] * members + cols_ref[...]
    sub = lax.broadcasted_iota(i32, (LANES, tiles), 0)
    value = jnp.where(sub < CAP, (where >> 3) - 4 * members // 8, where & 7)
    value = jnp.where((slot == (sub & (CAP - 1))) & (sub < 2 * CAP), value, 0)
    lab_ref[...] = lax.dot_general(
        named.astype(bf16), value.astype(f32).astype(bf16), (((1,), (1,)), ((), ())), preferred_element_type=f32
    )

    for k in range(kblocks):
        for c in range(BLOCK_ROWS):
            nat_ref[k, c : c + 1, :] = drive_ref[k : k + 1, c * LANES : (c + 1) * LANES]
        for c in range(ROWS):
            nat_ref[k, BLOCK_ROWS + c : BLOCK_ROWS + c + 1, :] = tau_ref[k : k + 1, c * LANES : (c + 1) * LANES]
    for k in range(kblocks):
        n0, n1, n2, t = (nat_ref[k, n * ROWS : (n + 1) * ROWS, :] for n in range(DIRS + 1))
        even = jnp.where(low, n0, turned(n1))
        odd = jnp.where(low, turned(n0), n1)
        du_ref[k, 0:ROWS, :] = even
        du_ref[k, ROWS : 2 * ROWS, :] = odd
        du_ref[k, 2 * ROWS :, :] = n2
        tu_ref[k, 0:ROWS, :] = jnp.where(low, t, turned(t))
        tu_ref[k, ROWS : 2 * ROWS, :] = jnp.where(low, turned(t), t)
        tu_ref[k, 2 * ROWS :, :] = t
        send_block(k, even, odd, n2, rows_ref.at[k], pk_ref)

    def block(d, carry):
        out_ref[d, TILE_ROWS:LABEL_AT, :] = pk_ref[sel_ref[d]]
        out_ref[d, LABEL_AT:FIRST_ROWS, :] = jnp.broadcast_to(lab_ref[pl.ds(d, 1), :], (8, LANES)).astype(bf16)
        return carry

    lax.fori_loop(0, members, block, 0, unroll=8)
    copy.wait()

    def move(i, carry):
        start = pl.multiple_of(slots_ref[0, i] * ROWS, ROWS)
        out_ref[dest_ref[i], pl.ds(start, ROWS), :] = rates_ref[i]
        return carry

    lax.fori_loop(0, tiles, move, 0, unroll=8)


def advance(last, op_ref, x_ref, x_at, sel_ref, drive_ref, tau_ref, out_ref, new_ref, rows_ref, prepare=None, chunks=1):
    members = x_ref.shape[0]
    kblocks = drive_ref.shape[0]
    low = low_half(ROWS)
    zero = jnp.zeros((), jnp.bfloat16)
    some = members // chunks
    total = None
    for q in range(chunks):
        if prepare is not None:
            prepare(q)
        entries = slice(q * some, (q + 1) * some)
        third = x_ref[entries, x_at + HALF : x_at + BLOCK_ROWS, :]
        third = jnp.concatenate([jnp.where(low, third, zero), jnp.where(low, zero, third)], axis=1)
        pair = x_ref[entries, x_at : x_at + HALF, :]
        right = jnp.concatenate([v.reshape(some * HALF, LANES) for v in (pair, third)], axis=1)
        left = op_ref[:, q * some * HALF : (q + 1) * some * HALF]
        part = jnp.dot(left, right, preferred_element_type=jnp.float32)
        total = part if total is None else total + part
    for r in range(kblocks):
        at = r * HALF
        pair = drive_ref[r, : 2 * ROWS, :] + tau_ref[r, : 2 * ROWS, :] * total[at : at + HALF, :LANES]
        even, odd = pair[:ROWS], pair[ROWS:]
        one = total[at : at + HALF, LANES:]
        one = one + turned(one)
        one = jnp.where(low, one[:ROWS], one[ROWS:])
        one = drive_ref[r, 2 * ROWS :, :] + tau_ref[r, 2 * ROWS :, :] * one
        if last:
            new_ref[r, 0:ROWS, :] = jnp.where(low, even, turned(odd))
            new_ref[r, ROWS : 2 * ROWS, :] = jnp.where(low, turned(even), odd)
            new_ref[r, 2 * ROWS :, :] = one
        else:
            send_block(r, even, odd, one, rows_ref.at[r], new_ref)
    if last:
        for k in range(kblocks):
            for c in range(BLOCK_ROWS):
                out_ref[k : k + 1, c * LANES : (c + 1) * LANES] = new_ref[k, c : c + 1, :]
    else:

        def block(d, carry):
            out_ref[d] = new_ref[sel_ref[d]]
            return carry

        lax.fori_loop(0, members, block, 0, unroll=8)


def first_kernel(sel_ref, x_ref, drive_ref, tau_ref, op_ref, out_ref, acc_ref, raw_ref, lab_ref, at_ref, pk_ref, rows_ref, sem):
    members = x_ref.shape[0]
    kblocks = drive_ref.shape[0]

    none = 4 * members

    def read(s, carry):
        raw_ref[pl.ds(s, 1), :] = x_ref[s, LABEL_AT:FIRST_ROWS, :].astype(jnp.float32)[0:1]
        return carry

    lax.fori_loop(0, members, read, 0, unroll=8)
    raw = raw_ref[...]
    place = (raw * 8.0 + pltpu.roll(raw, LANES - CAP, 1)).astype(jnp.int32) + none
    lab_ref[...] = place
    copy = pltpu.make_async_copy(lab_ref, at_ref, sem)
    copy.start()
    acc_ref[...] = jnp.zeros_like(acc_ref)
    copy.wait()

    def add(s, carry):
        ats = [at_ref[s, c] for c in range(CAP)]
        olds = [acc_ref[at] for at in ats]
        sums = []
        for c in range(CAP):
            same = jnp.zeros((ROWS, LANES), jnp.float32)
            for e in range(c):
                same = jnp.where(ats[e] == ats[c], sums[e], same)
            tile = x_ref[s, c * ROWS : (c + 1) * ROWS, :].astype(jnp.float32)
            sums.append(tile + same if c else tile)
        for c in range(CAP):
            acc_ref[ats[c]] = olds[c] + sums[c]
        return carry

    lax.fori_loop(0, members, add, 0, unroll=4)

    low = low_half(ROWS)

    pairs = members // 2 // 16

    def join(q):
        for g in range(q * pairs, (q + 1) * pairs):
            for r in range(kblocks):
                at = r * HALF
                a = acc_ref[r * members + 2 * g].astype(jnp.bfloat16)
                b = acc_ref[r * members + 2 * g + 1].astype(jnp.bfloat16)
                lanes = slice(g * LANES, (g + 1) * LANES)
                swap = turned(jnp.where(low, b, a))
                op_ref[at : at + ROWS, lanes] = jnp.where(low, a, swap)
                op_ref[at + ROWS : at + HALF, lanes] = jnp.where(low, swap, b)

    advance(False, op_ref, x_ref, TILE_ROWS, sel_ref, drive_ref, tau_ref, out_ref, pk_ref, rows_ref, join, 16)


def step_kernel(last, sel_ref, x_ref, op_ref, drive_ref, tau_ref, out_ref, new_ref, rows_ref):
    advance(last, op_ref, x_ref, 0, sel_ref, drive_ref, tau_ref, out_ref, new_ref, rows_ref, None, 16)


def shards(rates, tile_dest, tile_row, tile_col, send_list, drive, tau):
    members = lax.axis_size("pool") * lax.axis_size("ka")
    tiles = rates.shape[0]
    kblocks = drive.shape[0]
    exchange = functools.partial(lax.all_to_all, axis_name=AXES, split_axis=0, concat_axis=0, tiled=True)
    bf16, f32, i32 = jnp.bfloat16, jnp.float32, jnp.int32
    held = (kblocks, BLOCK_ROWS, LANES)
    rows = pltpu.VMEM((kblocks, HALF, LANES), f32)
    sel = send_list.reshape(members)

    first, drive_u, tau_u = pl.pallas_call(
        fill_kernel,
        out_shape=[
            jax.ShapeDtypeStruct((members, FIRST_ROWS, LANES), bf16),
            jax.ShapeDtypeStruct(held, f32),
            jax.ShapeDtypeStruct(held, f32),
        ],
        in_specs=[sspec()] * 2 + [vspec()] * 6,
        out_specs=[vspec()] * 3,
        scratch_shapes=[
            pltpu.VMEM((1, tiles), i32),
            pltpu.SMEM((1, tiles), i32),
            pltpu.VMEM((members, LANES), f32),
            pltpu.VMEM(held, bf16),
            pltpu.VMEM((kblocks, BLOCK_ROWS + ROWS, LANES), f32),
            rows,
            pltpu.SemaphoreType.DMA(()),
        ],
        compiler_params=params(16),
        name="fill",
    )(
        tile_dest[:, 0],
        sel,
        tile_dest.reshape(1, tiles),
        tile_row.reshape(1, tiles),
        tile_col.reshape(1, tiles),
        rates.reshape(tiles, ROWS, LANES),
        drive,
        tau,
    )
    first = exchange(first)

    operator, send = pl.pallas_call(
        first_kernel,
        out_shape=[
            jax.ShapeDtypeStruct((kblocks * HALF, members * HALF), bf16),
            jax.ShapeDtypeStruct((members, BLOCK_ROWS, LANES), bf16),
        ],
        in_specs=[sspec()] + [vspec()] * 3,
        out_specs=[vspec()] * 2,
        scratch_shapes=[
            pltpu.VMEM((kblocks * members + 1, ROWS, LANES), f32),
            pltpu.VMEM((members, LANES), f32),
            pltpu.VMEM((members, LANES), i32),
            pltpu.SMEM((members, LANES), i32),
            pltpu.VMEM(held, bf16),
            rows,
            pltpu.SemaphoreType.DMA(()),
        ],
        compiler_params=params(32),
        name="first",
    )(sel, first, drive_u, tau_u)

    for sweep in range(1, ITERS):
        last = sweep == ITERS - 1
        send = pl.pallas_call(
            functools.partial(step_kernel, last),
            out_shape=jax.ShapeDtypeStruct(drive.shape if last else send.shape, f32 if last else bf16),
            in_specs=[sspec()] + [vspec()] * 4,
            out_specs=vspec(),
            scratch_shapes=[pltpu.VMEM(held, f32 if last else bf16), rows],
            compiler_params=params(20),
            name="step_last" if last else "step",
        )(sel, exchange(send), operator, drive_u, tau_u)
    return send


def solution(mesh):
    pair = P(AXES, None)
    placed = (pair, pair, P(AXES), P(AXES), pair, pair, pair)
    return jax.shard_map(shards, mesh=mesh, in_specs=placed, out_specs=pair, check_vma=False)
```

```python
import functools

import jax
import jax.numpy as jnp
from jax import lax
from jax.experimental import pallas as pl
from jax.experimental.pallas import tpu as pltpu
from jax.sharding import PartitionSpec as P

ROWS = 32
LANES = 128
HALF = 64
ITERS = 3
CAP = 4
DIRS = 3
AXES = ("pool", "ka")
TILE_ROWS = CAP * ROWS
BLOCK_ROWS = DIRS * ROWS
LABEL_AT = TILE_ROWS + BLOCK_ROWS
FIRST_ROWS = LABEL_AT + 8

VMEM = pltpu.MemorySpace.VMEM
SMEM = pltpu.MemorySpace.SMEM


def vspec():
    return pl.BlockSpec(memory_space=VMEM)


def sspec():
    return pl.BlockSpec(memory_space=SMEM)


def params(mib):
    return pltpu.CompilerParams(vmem_limit_bytes=mib << 20)


def turned(value):
    return pltpu.roll(value, HALF, 1)


def low_half(rows):
    return lax.broadcasted_iota(jnp.int32, (rows, LANES), 1) < HALF


def send_block(k, even, odd, natural, rows_ref, pk_ref):
    low = low_half(ROWS)
    rows_ref[pl.ds(0, ROWS, stride=2), :] = even
    rows_ref[pl.ds(1, ROWS, stride=2), :] = odd
    pk_ref[k, :HALF, :] = rows_ref[...].astype(jnp.bfloat16)
    rows_ref[pl.ds(0, ROWS, stride=2), :] = natural
    rows_ref[pl.ds(1, ROWS, stride=2), :] = turned(natural)
    pk_ref[k, HALF:, :] = jnp.where(low, rows_ref[:ROWS, :], turned(rows_ref[ROWS:, :])).astype(jnp.bfloat16)


def fill_kernel(
    dest_ref, sel_ref, dests_ref, tile_rows_ref, cols_ref, rates_ref, drive_ref, tau_ref, out_ref, du_ref, tu_ref,
    slot_ref, slots_ref, lab_ref, pk_ref, nat_ref, rows_ref, sem,
):
    members = out_ref.shape[0]
    tiles = rates_ref.shape[0]
    kblocks = drive_ref.shape[0]
    f32, bf16, i32 = jnp.float32, jnp.bfloat16, jnp.int32
    low = low_half(ROWS)

    named = (lax.broadcasted_iota(i32, (members, tiles), 0) == dests_ref[...]).astype(f32)
    i0 = lax.broadcasted_iota(i32, (tiles, tiles), 0)
    i1 = lax.broadcasted_iota(i32, (tiles, tiles), 1)
    earlier = jnp.dot(named.astype(bf16), (i0 < i1).astype(f32).astype(bf16), preferred_element_type=f32)
    slot = jnp.sum(named * earlier, axis=0, keepdims=True).astype(i32)
    slot_ref[...] = slot
    copy = pltpu.make_async_copy(slot_ref, slots_ref, sem)
    copy.start()
    where = tile_rows_ref[...] * members + cols_ref[...]
    sub = lax.broadcasted_iota(i32, (LANES, tiles), 0)
    value = jnp.where(sub < CAP, (where >> 3) - 4 * members // 8, where & 7)
    value = jnp.where((slot == (sub & (CAP - 1))) & (sub < 2 * CAP), value, 0)
    lab_ref[...] = lax.dot_general(
        named.astype(bf16), value.astype(f32).astype(bf16), (((1,), (1,)), ((), ())), preferred_element_type=f32
    )

    for k in range(kblocks):
        for c in range(BLOCK_ROWS):
            nat_ref[k, c : c + 1, :] = drive_ref[k : k + 1, c * LANES : (c + 1) * LANES]
        for c in range(ROWS):
            nat_ref[k, BLOCK_ROWS + c : BLOCK_ROWS + c + 1, :] = tau_ref[k : k + 1, c * LANES : (c + 1) * LANES]
    for k in range(kblocks):
        n0, n1, n2, t = (nat_ref[k, n * ROWS : (n + 1) * ROWS, :] for n in range(DIRS + 1))
        even = jnp.where(low, n0, turned(n1))
        odd = jnp.where(low, turned(n0), n1)
        du_ref[k, 0:ROWS, :] = even
        du_ref[k, ROWS : 2 * ROWS, :] = odd
        du_ref[k, 2 * ROWS :, :] = n2
        tu_ref[k, 0:ROWS, :] = jnp.where(low, t, turned(t))
        tu_ref[k, ROWS : 2 * ROWS, :] = jnp.where(low, turned(t), t)
        tu_ref[k, 2 * ROWS :, :] = t
        send_block(k, even, odd, n2, rows_ref.at[k], pk_ref)

    def block(d, carry):
        out_ref[d, TILE_ROWS:LABEL_AT, :] = pk_ref[sel_ref[d]]
        out_ref[d, LABEL_AT:FIRST_ROWS, :] = jnp.broadcast_to(lab_ref[pl.ds(d, 1), :], (8, LANES)).astype(bf16)
        return carry

    lax.fori_loop(0, members, block, 0, unroll=8)
    copy.wait()

    def move(i, carry):
        start = pl.multiple_of(slots_ref[0, i] * ROWS, ROWS)
        out_ref[dest_ref[i], pl.ds(start, ROWS), :] = rates_ref[i]
        return carry

    lax.fori_loop(0, tiles, move, 0, unroll=16)


def advance(last, op_ref, x_ref, x_at, sel_ref, drive_ref, tau_ref, out_ref, new_ref, rows_ref, prepare=None, chunks=1):
    members = x_ref.shape[0]
    kblocks = drive_ref.shape[0]
    low = low_half(ROWS)
    zero = jnp.zeros((), jnp.bfloat16)
    some = members // chunks
    total = None
    for q in range(chunks):
        if prepare is not None:
            prepare(q)
        entries = slice(q * some, (q + 1) * some)
        third = x_ref[entries, x_at + HALF : x_at + BLOCK_ROWS, :]
        third = jnp.concatenate([jnp.where(low, third, zero), jnp.where(low, zero, third)], axis=1)
        pair = x_ref[entries, x_at : x_at + HALF, :]
        right = jnp.concatenate([v.reshape(some * HALF, LANES) for v in (pair, third)], axis=1)
        left = op_ref[:, q * some * HALF : (q + 1) * some * HALF]
        part = jnp.dot(left, right, preferred_element_type=jnp.float32)
        total = part if total is None else total + part
    for r in range(kblocks):
        at = r * HALF
        pair = drive_ref[r, : 2 * ROWS, :] + tau_ref[r, : 2 * ROWS, :] * total[at : at + HALF, :LANES]
        even, odd = pair[:ROWS], pair[ROWS:]
        one = total[at : at + HALF, LANES:]
        one = one + turned(one)
        one = jnp.where(low, one[:ROWS], one[ROWS:])
        one = drive_ref[r, 2 * ROWS :, :] + tau_ref[r, 2 * ROWS :, :] * one
        if last:
            new_ref[r, 0:ROWS, :] = jnp.where(low, even, turned(odd))
            new_ref[r, ROWS : 2 * ROWS, :] = jnp.where(low, turned(even), odd)
            new_ref[r, 2 * ROWS :, :] = one
        else:
            send_block(r, even, odd, one, rows_ref.at[r], new_ref)
    if last:
        for k in range(kblocks):
            for c in range(BLOCK_ROWS):
                out_ref[k : k + 1, c * LANES : (c + 1) * LANES] = new_ref[k, c : c + 1, :]
    else:

        def block(d, carry):
            out_ref[d] = new_ref[sel_ref[d]]
            return carry

        lax.fori_loop(0, members, block, 0, unroll=8)


def first_kernel(sel_ref, x_ref, drive_ref, tau_ref, op_ref, out_ref, acc_ref, raw_ref, lab_ref, at_ref, pk_ref, rows_ref, sem):
    members = x_ref.shape[0]
    kblocks = drive_ref.shape[0]

    none = 4 * members

    def read(s, carry):
        raw_ref[pl.ds(s, 1), :] = x_ref[s, LABEL_AT:FIRST_ROWS, :].astype(jnp.float32)[0:1]
        return carry

    lax.fori_loop(0, members, read, 0, unroll=8)
    raw = raw_ref[...]
    place = (raw * 8.0 + pltpu.roll(raw, LANES - CAP, 1)).astype(jnp.int32) + none
    lab_ref[...] = place
    copy = pltpu.make_async_copy(lab_ref, at_ref, sem)
    copy.start()
    acc_ref[...] = jnp.zeros_like(acc_ref)
    copy.wait()

    def add(s, carry):
        ats = [at_ref[s, c] for c in range(CAP)]
        olds = [acc_ref[at] for at in ats]
        sums = []
        for c in range(CAP):
            same = jnp.zeros((ROWS, LANES), jnp.float32)
            for e in range(c):
                same = jnp.where(ats[e] == ats[c], sums[e], same)
            tile = x_ref[s, c * ROWS : (c + 1) * ROWS, :].astype(jnp.float32)
            sums.append(tile + same if c else tile)
        for c in range(CAP):
            acc_ref[ats[c]] = olds[c] + sums[c]
        return carry

    lax.fori_loop(0, members, add, 0, unroll=8)

    low = low_half(ROWS)

    pairs = members // 2 // 16

    def join(q):
        for g in range(q * pairs, (q + 1) * pairs):
            for r in range(kblocks):
                at = r * HALF
                a = acc_ref[r * members + 2 * g].astype(jnp.bfloat16)
                b = acc_ref[r * members + 2 * g + 1].astype(jnp.bfloat16)
                lanes = slice(g * LANES, (g + 1) * LANES)
                swap = turned(jnp.where(low, b, a))
                op_ref[at : at + ROWS, lanes] = jnp.where(low, a, swap)
                op_ref[at + ROWS : at + HALF, lanes] = jnp.where(low, swap, b)

    advance(False, op_ref, x_ref, TILE_ROWS, sel_ref, drive_ref, tau_ref, out_ref, pk_ref, rows_ref, join, 16)


def step_kernel(last, sel_ref, x_ref, op_ref, drive_ref, tau_ref, out_ref, new_ref, rows_ref):
    advance(last, op_ref, x_ref, 0, sel_ref, drive_ref, tau_ref, out_ref, new_ref, rows_ref, None, 16)


def shards(rates, tile_dest, tile_row, tile_col, send_list, drive, tau):
    members = lax.axis_size("pool") * lax.axis_size("ka")
    tiles = rates.shape[0]
    kblocks = drive.shape[0]
    exchange = functools.partial(lax.all_to_all, axis_name=AXES, split_axis=0, concat_axis=0, tiled=True)
    bf16, f32, i32 = jnp.bfloat16, jnp.float32, jnp.int32
    held = (kblocks, BLOCK_ROWS, LANES)
    rows = pltpu.VMEM((kblocks, HALF, LANES), f32)
    sel = send_list.reshape(members)

    first, drive_u, tau_u = pl.pallas_call(
        fill_kernel,
        out_shape=[
            jax.ShapeDtypeStruct((members, FIRST_ROWS, LANES), bf16),
            jax.ShapeDtypeStruct(held, f32),
            jax.ShapeDtypeStruct(held, f32),
        ],
        in_specs=[sspec()] * 2 + [vspec()] * 6,
        out_specs=[vspec()] * 3,
        scratch_shapes=[
            pltpu.VMEM((1, tiles), i32),
            pltpu.SMEM((1, tiles), i32),
            pltpu.VMEM((members, LANES), f32),
            pltpu.VMEM(held, bf16),
            pltpu.VMEM((kblocks, BLOCK_ROWS + ROWS, LANES), f32),
            rows,
            pltpu.SemaphoreType.DMA(()),
        ],
        compiler_params=params(16),
        name="fill",
    )(
        tile_dest[:, 0],
        sel,
        tile_dest.reshape(1, tiles),
        tile_row.reshape(1, tiles),
        tile_col.reshape(1, tiles),
        rates.reshape(tiles, ROWS, LANES),
        drive,
        tau,
    )
    first = exchange(first)

    operator, send = pl.pallas_call(
        first_kernel,
        out_shape=[
            jax.ShapeDtypeStruct((kblocks * HALF, members * HALF), bf16),
            jax.ShapeDtypeStruct((members, BLOCK_ROWS, LANES), bf16),
        ],
        in_specs=[sspec()] + [vspec()] * 3,
        out_specs=[vspec()] * 2,
        scratch_shapes=[
            pltpu.VMEM((kblocks * members + 1, ROWS, LANES), f32),
            pltpu.VMEM((members, LANES), f32),
            pltpu.VMEM((members, LANES), i32),
            pltpu.SMEM((members, LANES), i32),
            pltpu.VMEM(held, bf16),
            rows,
            pltpu.SemaphoreType.DMA(()),
        ],
        compiler_params=params(32),
        name="first",
    )(sel, first, drive_u, tau_u)

    for sweep in range(1, ITERS):
        last = sweep == ITERS - 1
        send = pl.pallas_call(
            functools.partial(step_kernel, last),
            out_shape=jax.ShapeDtypeStruct(drive.shape if last else send.shape, f32 if last else bf16),
            in_specs=[sspec()] + [vspec()] * 4,
            out_specs=vspec(),
            scratch_shapes=[pltpu.VMEM(held, f32 if last else bf16), rows],
            compiler_params=params(20),
            name="step_last" if last else "step",
        )(sel, exchange(send), operator, drive_u, tau_u)
    return send


def solution(mesh):
    pair = P(AXES, None)
    placed = (pair, pair, P(AXES), P(AXES), pair, pair, pair)
    return jax.shard_map(shards, mesh=mesh, in_specs=placed, out_specs=pair, check_vma=False)
```

```python
import functools

import jax
import jax.numpy as jnp
from jax import lax
from jax.experimental import pallas as pl
from jax.experimental.pallas import tpu as pltpu
from jax.sharding import PartitionSpec as P

ROWS = 32
LANES = 128
HALF = 64
ITERS = 3
CAP = 4
DIRS = 3
AXES = ("pool", "ka")
TILE_ROWS = CAP * ROWS
BLOCK_ROWS = DIRS * ROWS
LABEL_AT = TILE_ROWS + BLOCK_ROWS
FIRST_ROWS = LABEL_AT + 8

VMEM = pltpu.MemorySpace.VMEM
SMEM = pltpu.MemorySpace.SMEM


def vspec():
    return pl.BlockSpec(memory_space=VMEM)


def sspec():
    return pl.BlockSpec(memory_space=SMEM)


def params(mib):
    return pltpu.CompilerParams(vmem_limit_bytes=mib << 20)


def turned(value):
    return pltpu.roll(value, HALF, 1)


def low_half(rows):
    return lax.broadcasted_iota(jnp.int32, (rows, LANES), 1) < HALF


def send_block(k, even, odd, natural, rows_ref, pk_ref):
    low = low_half(ROWS)
    rows_ref[pl.ds(0, ROWS, stride=2), :] = even
    rows_ref[pl.ds(1, ROWS, stride=2), :] = odd
    pk_ref[k, :HALF, :] = rows_ref[...].astype(jnp.bfloat16)
    rows_ref[pl.ds(0, ROWS, stride=2), :] = natural
    rows_ref[pl.ds(1, ROWS, stride=2), :] = turned(natural)
    pk_ref[k, HALF:, :] = jnp.where(low, rows_ref[:ROWS, :], turned(rows_ref[ROWS:, :])).astype(jnp.bfloat16)


def fill_kernel(
    dest_ref, sel_ref, dests_ref, tile_rows_ref, cols_ref, rates_ref, drive_ref, tau_ref, out_ref, du_ref, tu_ref,
    slot_ref, slots_ref, lab_ref, pk_ref, nat_ref, rows_ref, sem,
):
    members = out_ref.shape[0]
    tiles = rates_ref.shape[0]
    kblocks = drive_ref.shape[0]
    f32, bf16, i32 = jnp.float32, jnp.bfloat16, jnp.int32
    low = low_half(ROWS)

    named = (lax.broadcasted_iota(i32, (members, tiles), 0) == dests_ref[...]).astype(f32)
    i0 = lax.broadcasted_iota(i32, (tiles, tiles), 0)
    i1 = lax.broadcasted_iota(i32, (tiles, tiles), 1)
    earlier = jnp.dot(named.astype(bf16), (i0 < i1).astype(f32).astype(bf16), preferred_element_type=f32)
    slot = jnp.sum(named * earlier, axis=0, keepdims=True).astype(i32)
    slot_ref[...] = slot
    copy = pltpu.make_async_copy(slot_ref, slots_ref, sem)
    copy.start()
    where = tile_rows_ref[...] * members + cols_ref[...]
    sub = lax.broadcasted_iota(i32, (LANES, tiles), 0)
    value = jnp.where(sub < CAP, (where >> 3) - 4 * members // 8, where & 7)
    value = jnp.where((slot == (sub & (CAP - 1))) & (sub < 2 * CAP), value, 0)
    lab_ref[...] = lax.dot_general(
        named.astype(bf16), value.astype(f32).astype(bf16), (((1,), (1,)), ((), ())), preferred_element_type=f32
    )

    for k in range(kblocks):
        for c in range(BLOCK_ROWS):
            nat_ref[k, c : c + 1, :] = drive_ref[k : k + 1, c * LANES : (c + 1) * LANES]
        for c in range(ROWS):
            nat_ref[k, BLOCK_ROWS + c : BLOCK_ROWS + c + 1, :] = tau_ref[k : k + 1, c * LANES : (c + 1) * LANES]
    for k in range(kblocks):
        n0, n1, n2, t = (nat_ref[k, n * ROWS : (n + 1) * ROWS, :] for n in range(DIRS + 1))
        even = jnp.where(low, n0, turned(n1))
        odd = jnp.where(low, turned(n0), n1)
        du_ref[k, 0:ROWS, :] = even
        du_ref[k, ROWS : 2 * ROWS, :] = odd
        du_ref[k, 2 * ROWS :, :] = n2
        tu_ref[k, 0:ROWS, :] = jnp.where(low, t, turned(t))
        tu_ref[k, ROWS : 2 * ROWS, :] = jnp.where(low, turned(t), t)
        tu_ref[k, 2 * ROWS :, :] = t
        send_block(k, even, odd, n2, rows_ref.at[k], pk_ref)

    def block(d, carry):
        out_ref[d, TILE_ROWS:LABEL_AT, :] = pk_ref[sel_ref[d]]
        out_ref[d, LABEL_AT:FIRST_ROWS, :] = jnp.broadcast_to(lab_ref[pl.ds(d, 1), :], (8, LANES)).astype(bf16)
        return carry

    lax.fori_loop(0, members, block, 0, unroll=16)
    copy.wait()

    def move(i, carry):
        start = pl.multiple_of(slots_ref[0, i] * ROWS, ROWS)
        out_ref[dest_ref[i], pl.ds(start, ROWS), :] = rates_ref[i]
        return carry

    lax.fori_loop(0, tiles, move, 0, unroll=16)


def advance(last, op_ref, x_ref, x_at, sel_ref, drive_ref, tau_ref, out_ref, new_ref, rows_ref, prepare=None, chunks=1):
    members = x_ref.shape[0]
    kblocks = drive_ref.shape[0]
    low = low_half(ROWS)
    zero = jnp.zeros((), jnp.bfloat16)
    some = members // chunks
    total = None
    for q in range(chunks):
        if prepare is not None:
            prepare(q)
        entries = slice(q * some, (q + 1) * some)
        third = x_ref[entries, x_at + HALF : x_at + BLOCK_ROWS, :]
        third = jnp.concatenate([jnp.where(low, third, zero), jnp.where(low, zero, third)], axis=1)
        pair = x_ref[entries, x_at : x_at + HALF, :]
        right = jnp.concatenate([v.reshape(some * HALF, LANES) for v in (pair, third)], axis=1)
        left = op_ref[:, q * some * HALF : (q + 1) * some * HALF]
        part = jnp.dot(left, right, preferred_element_type=jnp.float32)
        total = part if total is None else total + part
    for r in range(kblocks):
        at = r * HALF
        pair = drive_ref[r, : 2 * ROWS, :] + tau_ref[r, : 2 * ROWS, :] * total[at : at + HALF, :LANES]
        even, odd = pair[:ROWS], pair[ROWS:]
        one = total[at : at + HALF, LANES:]
        one = one + turned(one)
        one = jnp.where(low, one[:ROWS], one[ROWS:])
        one = drive_ref[r, 2 * ROWS :, :] + tau_ref[r, 2 * ROWS :, :] * one
        if last:
            new_ref[r, 0:ROWS, :] = jnp.where(low, even, turned(odd))
            new_ref[r, ROWS : 2 * ROWS, :] = jnp.where(low, turned(even), odd)
            new_ref[r, 2 * ROWS :, :] = one
        else:
            send_block(r, even, odd, one, rows_ref.at[r], new_ref)
    if last:
        for k in range(kblocks):
            for c in range(BLOCK_ROWS):
                out_ref[k : k + 1, c * LANES : (c + 1) * LANES] = new_ref[k, c : c + 1, :]
    else:

        def block(d, carry):
            out_ref[d] = new_ref[sel_ref[d]]
            return carry

        lax.fori_loop(0, members, block, 0, unroll=16)


def first_kernel(sel_ref, x_ref, drive_ref, tau_ref, op_ref, out_ref, acc_ref, raw_ref, lab_ref, at_ref, pk_ref, rows_ref, sem):
    members = x_ref.shape[0]
    kblocks = drive_ref.shape[0]

    none = 4 * members

    def read(s, carry):
        raw_ref[pl.ds(s, 1), :] = x_ref[s, LABEL_AT:FIRST_ROWS, :].astype(jnp.float32)[0:1]
        return carry

    lax.fori_loop(0, members, read, 0, unroll=8)
    raw = raw_ref[...]
    place = (raw * 8.0 + pltpu.roll(raw, LANES - CAP, 1)).astype(jnp.int32) + none
    lab_ref[...] = place
    copy = pltpu.make_async_copy(lab_ref, at_ref, sem)
    copy.start()
    acc_ref[...] = jnp.zeros_like(acc_ref)
    copy.wait()

    def add(s, carry):
        ats = [at_ref[s, c] for c in range(CAP)]
        olds = [acc_ref[at] for at in ats]
        sums = []
        for c in range(CAP):
            same = jnp.zeros((ROWS, LANES), jnp.float32)
            for e in range(c):
                same = jnp.where(ats[e] == ats[c], sums[e], same)
            tile = x_ref[s, c * ROWS : (c + 1) * ROWS, :].astype(jnp.float32)
            sums.append(tile + same if c else tile)
        for c in range(CAP):
            acc_ref[ats[c]] = olds[c] + sums[c]
        return carry

    lax.fori_loop(0, members, add, 0, unroll=16)

    low = low_half(ROWS)

    pairs = members // 2 // 16

    def join(q):
        for g in range(q * pairs, (q + 1) * pairs):
            for r in range(kblocks):
                at = r * HALF
                a = acc_ref[r * members + 2 * g].astype(jnp.bfloat16)
                b = acc_ref[r * members + 2 * g + 1].astype(jnp.bfloat16)
                lanes = slice(g * LANES, (g + 1) * LANES)
                swap = turned(jnp.where(low, b, a))
                op_ref[at : at + ROWS, lanes] = jnp.where(low, a, swap)
                op_ref[at + ROWS : at + HALF, lanes] = jnp.where(low, swap, b)

    advance(False, op_ref, x_ref, TILE_ROWS, sel_ref, drive_ref, tau_ref, out_ref, pk_ref, rows_ref, join, 16)


def step_kernel(last, sel_ref, x_ref, op_ref, drive_ref, tau_ref, out_ref, new_ref, rows_ref):
    advance(last, op_ref, x_ref, 0, sel_ref, drive_ref, tau_ref, out_ref, new_ref, rows_ref, None, 16)


def shards(rates, tile_dest, tile_row, tile_col, send_list, drive, tau):
    members = lax.axis_size("pool") * lax.axis_size("ka")
    tiles = rates.shape[0]
    kblocks = drive.shape[0]
    exchange = functools.partial(lax.all_to_all, axis_name=AXES, split_axis=0, concat_axis=0, tiled=True)
    bf16, f32, i32 = jnp.bfloat16, jnp.float32, jnp.int32
    held = (kblocks, BLOCK_ROWS, LANES)
    rows = pltpu.VMEM((kblocks, HALF, LANES), f32)
    sel = send_list.reshape(members)

    first, drive_u, tau_u = pl.pallas_call(
        fill_kernel,
        out_shape=[
            jax.ShapeDtypeStruct((members, FIRST_ROWS, LANES), bf16),
            jax.ShapeDtypeStruct(held, f32),
            jax.ShapeDtypeStruct(held, f32),
        ],
        in_specs=[sspec()] * 2 + [vspec()] * 6,
        out_specs=[vspec()] * 3,
        scratch_shapes=[
            pltpu.VMEM((1, tiles), i32),
            pltpu.SMEM((1, tiles), i32),
            pltpu.VMEM((members, LANES), f32),
            pltpu.VMEM(held, bf16),
            pltpu.VMEM((kblocks, BLOCK_ROWS + ROWS, LANES), f32),
            rows,
            pltpu.SemaphoreType.DMA(()),
        ],
        compiler_params=params(16),
        name="fill",
    )(
        tile_dest[:, 0],
        sel,
        tile_dest.reshape(1, tiles),
        tile_row.reshape(1, tiles),
        tile_col.reshape(1, tiles),
        rates.reshape(tiles, ROWS, LANES),
        drive,
        tau,
    )
    first = exchange(first)

    operator, send = pl.pallas_call(
        first_kernel,
        out_shape=[
            jax.ShapeDtypeStruct((kblocks * HALF, members * HALF), bf16),
            jax.ShapeDtypeStruct((members, BLOCK_ROWS, LANES), bf16),
        ],
        in_specs=[sspec()] + [vspec()] * 3,
        out_specs=[vspec()] * 2,
        scratch_shapes=[
            pltpu.VMEM((kblocks * members + 1, ROWS, LANES), f32),
            pltpu.VMEM((members, LANES), f32),
            pltpu.VMEM((members, LANES), i32),
            pltpu.SMEM((members, LANES), i32),
            pltpu.VMEM(held, bf16),
            rows,
            pltpu.SemaphoreType.DMA(()),
        ],
        compiler_params=params(32),
        name="first",
    )(sel, first, drive_u, tau_u)

    for sweep in range(1, ITERS):
        last = sweep == ITERS - 1
        send = pl.pallas_call(
            functools.partial(step_kernel, last),
            out_shape=jax.ShapeDtypeStruct(drive.shape if last else send.shape, f32 if last else bf16),
            in_specs=[sspec()] + [vspec()] * 4,
            out_specs=vspec(),
            scratch_shapes=[pltpu.VMEM(held, f32 if last else bf16), rows],
            compiler_params=params(20),
            name="step_last" if last else "step",
        )(sel, exchange(send), operator, drive_u, tau_u)
    return send


def solution(mesh):
    pair = P(AXES, None)
    placed = (pair, pair, P(AXES), P(AXES), pair, pair, pair)
    return jax.shard_map(shards, mesh=mesh, in_specs=placed, out_specs=pair, check_vma=False)
```
